32 devices in a mesh: rows: 4 (over y, x), wide: 8 (over z, core).
Axes of the slice: x: 2, y: 2, z: 4, core: 2. Of those that a mesh axis runs over, the one named last changes fastest.
Arguments:
- block_input: bfloat16 [4, 1024, 2048], P('rows', 'wide'), may hold values from -6 to 6
- out_grad: bfloat16 [4, 1024, 2048], P('rows', 'wide'), may hold values from -6 to 6
- segment_ids: int32 [4, 1024], P('rows'), may hold values from 0 to 7, as said below
- positions: int32 [4, 1024], P('rows', 'wide'), may hold values from 0 to 511, as said below
- norm_params: bfloat16 [4, 2048], P(None, ('rows', 'wide')), may hold values from -0.7 to 1.525
- w_qkv: bfloat16 [2048, 6144], P(('rows', 'wide')), may hold values from -0.125 to 0.125
- b_qkv: bfloat16 [6144], P(('rows', 'wide')), may hold values from -1.1953125 to 1.1953125
- w_out: bfloat16 [2048, 2048], P(('rows', 'wide')), may hold values from -1 to 1
- gate_up: bfloat16 [2, 2048, 5632], P(None, 'rows', 'wide'), may hold values from -0.125 to 0.125
- w_down: bfloat16 [5632, 2048], P('wide', 'rows'), may hold values from -0.078125 to 0.078125
- moment_norm: float32 [2, 4, 2048], P(None, None, ('rows', 'wide')), may hold values from -175 to 40000, as said below
- moment_qkv: float32 [2, 2048, 6144], P(None, ('rows', 'wide')), may hold values from -175 to 40000, as said below
- moment_bias: float32 [2, 6144], P(None, ('rows', 'wide')), may hold values from -175 to 40000, as said below
- moment_out: float32 [2, 2048, 2048], P(None, ('rows', 'wide')), may hold values from -175 to 40000, as said below
- moment_gate: float32 [2, 2, 2048, 5632], P(None, None, 'rows', 'wide'), may hold values from -175 to 40000, as said below
- moment_down: float32 [2, 5632, 2048], P(None, 'wide', 'rows'), may hold values from -175 to 40000, as said below
Outputs:
- block_output: bfloat16 [4, 1024, 2048], P('rows', 'wide')
- input_grad: float32 [4, 1024, 2048], P('rows', 'wide')
- grad_norms: float32 [4, 2048], P(None, ('rows', 'wide'))
- grad_qkv: float32 [2048, 6144], P(('rows', 'wide'))
- grad_bias: float32 [6144], P(('rows', 'wide'))
- grad_out: float32 [2048, 2048], P(('rows', 'wide'))
- grad_gate: float32 [2, 2048, 5632], P(None, 'rows', 'wide')
- grad_down: float32 [5632, 2048], P('wide', 'rows')
- step_norms: float32 [4, 2048], P(None, ('rows', 'wide'))
- step_qkv: float32 [2048, 6144], P(('rows', 'wide'))
- step_bias: float32 [6144], P(('rows', 'wide'))
- step_out: float32 [2048, 2048], P(('rows', 'wide'))
- step_gate: float32 [2, 2048, 5632], P(None, 'rows', 'wide')
- step_down: float32 [5632, 2048], P('wide', 'rows')
The draws below stay inside these ranges and needn't reach their ends.
Inputs may be any that keep to these rules, and one draw needn't show every extreme that they name: `segment_ids`: within a row segment ids never fall, and every one of 0 to 7 occurs. positions[b, i] is i minus the index of the first token of the document of token i in row b. `moment_norm`: index 1 of the first dimension holds second moments, from 625 to 40000. `moment_qkv`: index 1 of the first dimension holds second moments, from 625 to 40000. `moment_bias`: index 1 of the first dimension holds second moments, from 625 to 40000. `moment_out`: index 1 of the first dimension holds second moments, from 625 to 40000. `moment_gate`: index 1 of the first dimension holds second moments, from 625 to 40000. `moment_down`: index 1 of the first dimension holds second moments, from 625 to 40000.
All inputs are finite; a program needn't handle non-finite values.
Results may differ from the reference program's by a relative error of at most 0.014.
Values may be sent and summed in bfloat16 or wider, within the bound.
No kernel may reach another device: no remote copies, remote signals or barrier semaphores. Data moves between devices by JAX's collectives and lax.ppermute only.
A program may use at most 256 MiB of HBM per device.

```python
import math
import jax
import jax.numpy as jnp
from jax import lax

D = 2048
HEADS = 32
HEAD_DIM = 64
ROT_DIMS = 16
FF = 5632
DOCS = 8
SEQ = 1024
BATCH = 4


def packed_documents(key):
    row_keys = jax.random.split(jax.random.fold_in(key, 11), BATCH)
    long_len = SEQ // 2
    rest_len = SEQ - long_len

    def one_row(row_key):
        perm_key, place_key = jax.random.split(row_key)
        shuffled = jax.random.permutation(perm_key, rest_len - 1)
        inner_cuts = jnp.sort(shuffled[:DOCS - 2] + 1).astype(jnp.int32)
        bounds = jnp.concatenate([jnp.zeros((1,), jnp.int32), inner_cuts, jnp.full((1,), rest_len, jnp.int32)])
        others = bounds[1:] - bounds[:-1]
        long_index = jax.random.randint(place_key, (), 0, DOCS).astype(jnp.int32)
        doc_index = jnp.arange(DOCS, dtype=jnp.int32)
        pick = jnp.clip(jnp.where(doc_index > long_index, doc_index - 1, doc_index), 0, DOCS - 2)
        lengths = jnp.where(doc_index == long_index, long_len, others[pick]).astype(jnp.int32)
        ends = jnp.cumsum(lengths).astype(jnp.int32)
        cut_points = ends[:DOCS - 1]
        indices = jnp.arange(SEQ, dtype=jnp.int32)
        passed = cut_points[None, :] <= indices[:, None]
        segment = jnp.sum(passed.astype(jnp.int32), axis=1)
        starts = jnp.max(jnp.where(passed, cut_points[None, :], 0), axis=1)
        return (segment, indices - starts)
    return jax.vmap(one_row)(row_keys)


def draw_segment_ids(key, part):
    return packed_documents(key)[0]


def draw_positions(key, part):
    return packed_documents(key)[1]


def draw_norm_params(key, part):
    own_key = jax.random.fold_in(key, 3)
    jitter = jnp.clip(jax.random.normal(own_key, (4, D), jnp.float32), -3.5, 3.5)
    gains_row = (jnp.arange(4) % 2 == 0)[:, None]
    return jnp.where(gains_row, 1.0 + 0.15 * jitter, 0.2 * jitter).astype(jnp.bfloat16)


def moment_pair(key, tag, shape):
    first_key, second_key = jax.random.split(jax.random.fold_in(key, tag))
    first_moment = 50.0 * jnp.clip(jax.random.normal(first_key, shape, jnp.float32), -3.5, 3.5)
    second_moment = jnp.exp(jax.random.uniform(second_key, shape, jnp.float32, math.log(625.0), math.log(40000.0)))
    return jnp.stack([first_moment, second_moment])


def draw_moment_norm(key, part):
    return moment_pair(key, 21, (4, D))


def draw_moment_qkv(key, part):
    return moment_pair(key, 22, (D, 3 * D))


def draw_moment_bias(key, part):
    return moment_pair(key, 23, (3 * D,))


def draw_moment_out(key, part):
    return moment_pair(key, 24, (D, D))


def draw_moment_gate(key, part):
    return moment_pair(key, 25, (2, D, FF))


def draw_moment_down(key, part):
    return moment_pair(key, 26, (FF, D))


def block_scale(key, dims, pieces, smallest, top_value):
    def one(axis_at, shards_of):
        draws = jax.random.uniform(jax.random.fold_in(jax.random.fold_in(key, 6), axis_at), (shards_of,), jnp.float32, smallest / len(pieces), top_value / len(pieces))
        return jnp.repeat(jnp.exp(draws), dims[axis_at] // shards_of).reshape((-1,) + (1,) * (len(dims) - axis_at - 1))

    gain = one(*pieces[0])
    for cut in pieces[1:]:
        gain = gain * one(*cut)
    return gain


def bell_draw(stream_key, shape, scale, limit, cuts=(), kind=jnp.bfloat16):
    array = scale * jax.random.normal(stream_key, shape, jnp.float32)
    if cuts:
        array = array * block_scale(stream_key, shape, cuts, -0.22, 0.18)
    return jnp.clip(array, -limit, limit).astype(kind)


def setup_inputs(seed: int = 0) -> dict:
    key_of = jax.random.split(jax.random.key(seed), 17)
    block_input = bell_draw(key_of[0], (BATCH, SEQ, D), 1.0, 6.0, ((0, 4), (1, 8)))
    out_grad = bell_draw(key_of[1], (BATCH, SEQ, D), 1.0, 6.0, ((0, 4), (1, 8)))
    segment_ids = draw_segment_ids(jax.random.fold_in(key_of[16], 71), 0)
    positions = draw_positions(jax.random.fold_in(key_of[16], 71), 0)
    norm_params = draw_norm_params(jax.random.fold_in(key_of[16], 71), 0)
    w_qkv = bell_draw(key_of[5], (D, 3 * D), D ** -0.5, 0.125, ((0, 32),))
    b_qkv = bell_draw(key_of[6], (3 * D,), 0.2, 1.1953125, ((0, 32),))
    w_out = bell_draw(key_of[7], (D, D), (D // 64) ** -0.5, 1.0, ((0, 32),))
    gate_up = bell_draw(key_of[8], (2, D, FF), D ** -0.5, 0.125, ((1, 4), (2, 8)))
    w_down = bell_draw(key_of[9], (FF, D), FF ** -0.5, 0.078125, ((0, 8), (1, 4)))
    moment_norm = draw_moment_norm(jax.random.fold_in(key_of[16], 71), 0)
    moment_qkv = draw_moment_qkv(jax.random.fold_in(key_of[16], 71), 0)
    moment_bias = draw_moment_bias(jax.random.fold_in(key_of[16], 71), 0)
    moment_out = draw_moment_out(jax.random.fold_in(key_of[16], 71), 0)
    moment_gate = draw_moment_gate(jax.random.fold_in(key_of[16], 71), 0)
    moment_down = draw_moment_down(jax.random.fold_in(key_of[16], 71), 0)
    return {"block_input": block_input, "out_grad": out_grad, "segment_ids": segment_ids, "positions": positions, "norm_params": norm_params, "w_qkv": w_qkv, "b_qkv": b_qkv, "w_out": w_out, "gate_up": gate_up, "w_down": w_down, "moment_norm": moment_norm, "moment_qkv": moment_qkv, "moment_bias": moment_bias, "moment_out": moment_out, "moment_gate": moment_gate, "moment_down": moment_down}


@jax.custom_vjp
def low(v):
    return lax.optimization_barrier(v.astype(jnp.bfloat16)).astype(jnp.float32)

@jax.custom_vjp
def low_back(v):
    return v

def low_keep(v):
    return (low(v), None)

def low_pass(kept, grad):
    return (grad,)

def back_keep(v):
    return (v, None)

def back_low(kept, grad):
    return (low(grad),)
low.defvjp(low_keep, low_pass)
low_back.defvjp(back_keep, back_low)
NORM_EPS = 1e-05
NEG_LARGE = -1e+30
SCORE_SCALE = 0.125
ROPE_BASE = 10000.0
BETA_ONE = 0.9
BETA_TWO = 0.95
BIAS_FIRST = 0.999973438601112
BIAS_SECOND = 0.994079470779667
ADAM_EPS = 1e-08
DECAY_RATE = 0.1
PRECISE = lax.Precision.HIGHEST

def rotary_tables(positions):
    half_dims = ROT_DIMS // 2
    frequency = jnp.exp(jnp.arange(half_dims, dtype=jnp.float32) * (-2.0 * jnp.log(ROPE_BASE) / ROT_DIMS))
    angles = positions.astype(jnp.float32)[:, None] * frequency[None, :]
    return (jnp.cos(angles)[:, None, :], jnp.sin(angles)[:, None, :])

def rotate(tensor, cosine, sine_part):
    half_dims = ROT_DIMS // 2
    leading = tensor[..., :half_dims]
    trailing = tensor[..., half_dims:ROT_DIMS]
    return jnp.concatenate([leading * cosine - trailing * sine_part, trailing * cosine + leading * sine_part, tensor[..., ROT_DIMS:]], axis=-1)

def layer_norm(tensor, norm_gain, norm_shift):
    center = tensor - lax.optimization_barrier(jnp.mean(tensor, axis=-1, keepdims=True))
    inverse = lax.rsqrt(lax.optimization_barrier(jnp.mean(center * center, axis=-1, keepdims=True)) + NORM_EPS)
    return center * inverse * norm_gain + norm_shift

def visible(segment_row, query_first, query_amount, key_first, key_amount):
    query_seg = lax.dynamic_slice_in_dim(segment_row, query_first, query_amount)
    key_seg = lax.dynamic_slice_in_dim(segment_row, key_first, key_amount)
    query_pos = query_first + jnp.arange(query_amount, dtype=jnp.int32)
    key_pos = key_first + jnp.arange(key_amount, dtype=jnp.int32)
    return (query_seg[:, None] == key_seg[None, :]) & (key_pos[None, :] <= query_pos[:, None])

def forward_row(hidden_in, weights, segment_row, position_row):
    norm_vals, qkv_w, bias_w, out_w, gate_w, down_w = weights
    seq_len, model_width = hidden_in.shape
    normed_one = low(layer_norm(hidden_in, norm_vals[0], norm_vals[1]))
    projected = low_back(jnp.dot(normed_one, qkv_w, precision=PRECISE) + bias_w)
    cosine, sine_part = rotary_tables(position_row)
    shaped = (seq_len, HEADS, HEAD_DIM)
    queries = low(rotate(projected[:, :model_width].reshape(shaped), cosine, sine_part))
    keys_all = low(rotate(projected[:, model_width:2 * model_width].reshape(shaped), cosine, sine_part))
    values = low(projected[:, 2 * model_width:].reshape(shaped))
    block_len = min(512, seq_len)
    blocks = seq_len // block_len

    def attend_pair(operand):
        query_blk, query_first = operand
        scores = low_back(jnp.einsum('qhe,khe->hqk', query_blk, keys_all, precision=PRECISE) * SCORE_SCALE)
        allowed = visible(segment_row, query_first, block_len, 0, seq_len)
        attn_probs = low(jax.nn.softmax(jnp.where(allowed[None], scores, NEG_LARGE), axis=-1))
        return jnp.einsum('hqk,khe->qhe', attn_probs, values, precision=PRECISE)
    attended = lax.map(jax.checkpoint(attend_pair), (queries.reshape(blocks, block_len, HEADS, HEAD_DIM), jnp.arange(blocks, dtype=jnp.int32) * block_len))
    attended = low_back(low(attended.reshape(seq_len, model_width)))
    after_attn = hidden_in + low_back(jnp.dot(attended, out_w, precision=PRECISE))
    normed_two = low(layer_norm(after_attn, norm_vals[2], norm_vals[3]))
    gate_vals = low_back(jnp.einsum('td,gdf->gtf', normed_two, gate_w, precision=PRECISE))
    hidden = low(jax.nn.silu(gate_vals[0]) * gate_vals[1])
    return after_attn + low_back(jnp.dot(hidden, down_w, precision=PRECISE))

def adam_step(parameter, gradient, moments):
    first_moment = BETA_ONE * moments[0] + (1.0 - BETA_ONE) * gradient
    second_moment = BETA_TWO * moments[1] + (1.0 - BETA_TWO) * gradient * gradient
    return first_moment / BIAS_FIRST / (jnp.sqrt(second_moment / BIAS_SECOND) + ADAM_EPS) + DECAY_RATE * parameter

def reference(block_input, out_grad, segment_ids, positions, norm_params, w_qkv, b_qkv, w_out, gate_up, w_down, moment_norm, moment_qkv, moment_bias, moment_out, moment_gate, moment_down):
    params = (norm_params.astype(jnp.float32), w_qkv.astype(jnp.float32), b_qkv.astype(jnp.float32), w_out.astype(jnp.float32), gate_up.astype(jnp.float32), w_down.astype(jnp.float32))

    def row_step(totals, inputs):
        input_row, grad_row, segment_row, position_row = inputs

        def forward(hidden_in, weights):
            return forward_row(hidden_in, weights, segment_row, position_row)
        output_row, pullback = jax.vjp(forward, input_row.astype(jnp.float32), params)
        input_grad_row, row_grads = pullback(grad_row.astype(jnp.float32))
        totals = jax.tree.map(lambda earlier, later: earlier + later, totals, row_grads)
        return (totals, (output_row.astype(jnp.bfloat16), input_grad_row))
    zero_grads = jax.tree.map(jnp.zeros_like, params)
    weight_grads, (outputs, input_grads) = lax.scan(row_step, zero_grads, (block_input, out_grad, segment_ids, positions))
    moments = (moment_norm, moment_qkv, moment_bias, moment_out, moment_gate, moment_down)
    updates = jax.tree.map(adam_step, params, weight_grads, moments)
    return (outputs, input_grads, weight_grads[0], weight_grads[1], weight_grads[2], weight_grads[3], weight_grads[4], weight_grads[5], updates[0], updates[1], updates[2], updates[3], updates[4], updates[5])
```

```python
import functools

import jax
import jax.numpy as jnp
from jax import lax
from jax.experimental import pallas as pl
from jax.experimental.pallas import tpu as pltpu
from jax.sharding import PartitionSpec as P

F = jnp.float32
B = jnp.bfloat16
HEADS = 32
HEAD_DIM = 64
ROT_DIMS = 16
HALF_ROT = ROT_DIMS // 2
NORM_EPS = 1e-05
NEG_LARGE = -1e30
SCORE_SCALE = 0.125
ROPE_BASE = 10000.0
BETA_ONE = 0.9
BETA_TWO = 0.95
BIAS_FIRST = 0.999973438601112
BIAS_SECOND = 0.994079470779667
ADAM_EPS = 1e-08
DECAY_RATE = 0.1
TOKEN_BLOCK = 256
EXTRA_ROWS = 8
NT = (((1,), (1,)), ((), ()))
TN = (((0,), (0,)), ((), ()))


def dotg(left, right, dims):
    return lax.dot_general(left, right, dims, preferred_element_type=F)


def plus(left, right):
    return (left.astype(F) + right.astype(F)).astype(B)


def rows_swap(value, bits):
    return lax.ppermute(value, "rows", [(i, i ^ bits) for i in range(4)])


def rows_gather(shard, axis):
    if lax.axis_size("rows") != 4:
        return lax.all_gather(shard, "rows", axis=axis, tiled=True)
    me = lax.axis_index("rows")
    half = shard.shape[0] // 2
    near = rows_swap(shard, 1)
    far = rows_swap(shard, 2)
    diagonal = (rows_swap(near[:half], 2), rows_swap(far[half:], 1))
    shape = list(shard.shape)
    size = shape[axis]
    shape[axis] = 4 * size
    whole = jnp.zeros(shape, shard.dtype)
    for piece, bits, first in ((shard, 0, 0), (near, 1, 0), (far, 2, 0), (diagonal[0], 3, 0), (diagonal[1], 3, half)):
        start = [0] * len(shape)
        start[0] = first
        start[axis] = start[axis] + (me ^ bits) * size
        whole = lax.dynamic_update_slice(whole, piece, start)
    return whole


def rows_scatter(whole, axis):
    if lax.axis_size("rows") != 4:
        return lax.psum_scatter(whole, "rows", scatter_dimension=axis, tiled=True).astype(F)
    me = lax.axis_index("rows")
    size = whole.shape[axis] // 4
    part = lambda bits: lax.dynamic_slice_in_dim(whole, (me ^ bits) * size, size, axis)
    diagonal = part(3)
    half = diagonal.shape[0] // 2
    from_near = rows_swap(diagonal[:half], 1)
    from_far = rows_swap(diagonal[half:], 2)
    far = part(2)
    near = part(1)
    far = rows_swap(jnp.concatenate([plus(far[:half], from_near), far[half:]], 0), 2)
    near = rows_swap(jnp.concatenate([near[:half], plus(near[half:], from_far)], 0), 1)
    return part(0).astype(F) + far.astype(F) + near.astype(F)


def wide_exchange(blocks):
    count = lax.axis_size("wide")
    me = lax.axis_index("wide")
    whole = jnp.zeros(blocks.shape, blocks.dtype)
    for step in range(count):
        block = lax.dynamic_slice_in_dim(blocks, (me + step) % count, 1, 0)
        if step:
            block = lax.ppermute(block, "wide", [(i, (i + step) % count) for i in range(count)])
        whole = lax.dynamic_update_slice_in_dim(whole, block, (me - step) % count, 0)
    return whole


def wide_gather(shard):
    return lax.all_gather(shard, "wide", axis=0, tiled=True)


def wide_scatter(whole):
    return lax.psum_scatter(whole, "wide", scatter_dimension=0, tiled=True).astype(F)


def rotated(value, same, ahead, behind):
    width = value.shape[1]
    return (
        value * same
        + pltpu.roll(value, width - HALF_ROT, 1) * ahead
        + pltpu.roll(value, HALF_ROT, 1) * behind
    )


def unrotated(value, same, ahead, behind):
    width = value.shape[1]
    return value * same - (
        pltpu.roll(value, width - HALF_ROT, 1) * ahead
        + pltpu.roll(value, HALF_ROT, 1) * behind
    )


def unit_rows(tensor):
    center = tensor - jnp.mean(tensor, axis=-1, keepdims=True)
    inverse = lax.rsqrt(jnp.mean(center * center, axis=-1, keepdims=True) + NORM_EPS)
    return center * inverse, inverse


def project_body(
    x_ref, norm_ref, w_ref, bias_ref, same_ref, ahead_ref, behind_ref, q_ref, k_ref, v_ref, normed_ref
):
    hat, _ = unit_rows(x_ref[...].astype(F))
    normed = (hat * norm_ref[0:1, :] + norm_ref[1:2, :]).astype(B)
    normed_ref[...] = normed
    out = jnp.dot(normed, w_ref[...], preferred_element_type=F) + bias_ref[...]
    width = q_ref.shape[1]
    tables = (same_ref[...], ahead_ref[...], behind_ref[...])
    q_ref[...] = rotated(out[:, :width], *tables).astype(B)
    k_ref[...] = rotated(out[:, width : 2 * width], *tables).astype(B)
    v_ref[...] = out[:, 2 * width :].astype(B)


def row_spec(width, block):
    return pl.BlockSpec((block, width), lambda i: (i, 0))


def whole_spec(array):
    return pl.BlockSpec(array.shape, lambda i: (0, 0))


def project(x_all, norm_one, w_mine, bias_mine, tables):
    tokens, features = x_all.shape
    width = w_mine.shape[1] // 3
    block = min(TOKEN_BLOCK, tokens)
    return pl.pallas_call(
        project_body,
        grid=(tokens // block,),
        in_specs=[
            row_spec(features, block),
            whole_spec(norm_one),
            whole_spec(w_mine),
            whole_spec(bias_mine),
        ]
        + [row_spec(width, block)] * 3,
        out_specs=[row_spec(width, block)] * 3 + [row_spec(features, block)],
        out_shape=[jax.ShapeDtypeStruct((tokens, width), B)] * 3
        + [jax.ShapeDtypeStruct((tokens, features), B)],
        name="project",
    )(x_all, norm_one, w_mine, bias_mine, *tables)


def pair_bias(seg_col, seg_row, first, size, keys):
    same = seg_col[first : first + size, :] == seg_row[:, :keys]
    key_pos = lax.broadcasted_iota(jnp.int32, (size, keys), 1)
    query_pos = first + lax.broadcasted_iota(jnp.int32, (size, keys), 0)
    return jnp.where(same & (key_pos <= query_pos), 0.0, NEG_LARGE)


def head_masks(heads, width):
    lane = lax.broadcasted_iota(jnp.int32, (1, width), 1) // HEAD_DIM
    return [jnp.where(lane == head, 1.0, 0.0).astype(B) for head in range(heads)]


def attend_body(heads, q_ref, k_ref, v_ref, seg_col, seg_row, out_ref, lse_ref):
    tokens, width = q_ref.shape
    block = min(TOKEN_BLOCK, tokens)
    masks = head_masks(heads, width)
    for first in range(0, tokens, block):
        keys = first + block
        bias = pair_bias(seg_col, seg_row, first, block, keys)
        queries = q_ref[first:keys, :]
        total = jnp.zeros((block, width), F)
        for head in range(heads):
            scores = dotg(queries * (masks[head] * SCORE_SCALE), k_ref[:keys, :], NT) + bias
            top = jnp.max(scores, axis=-1, keepdims=True)
            weights = jnp.exp(scores - top)
            norm = jnp.sum(weights, axis=-1, keepdims=True)
            probs = (weights * (1.0 / norm)).astype(B)
            total += jnp.dot(probs, v_ref[:keys, :] * masks[head], preferred_element_type=F)
            lse_ref[first:keys, head : head + 1] = top + jnp.log(norm)
        out_ref[first:keys, :] = total.astype(B)


def attend(q, k, v, seg_col, seg_row, heads):
    tokens, width = q.shape
    return pl.pallas_call(
        functools.partial(attend_body, heads),
        out_shape=[
            jax.ShapeDtypeStruct((tokens, width), B),
            jax.ShapeDtypeStruct((tokens, 128), F),
        ],
        name="attend",
    )(q, k, v, seg_col, seg_row)


def attend_back_body(
    heads, q_ref, k_ref, v_ref, g_ref, lse_ref, seg_col, seg_row, same_ref, ahead_ref, behind_ref,
    out_ref, bias_ref, dq_ref, dk_ref, dv_ref,
):
    tokens, width = q_ref.shape
    block = min(TOKEN_BLOCK, tokens)
    masks = head_masks(heads, width)
    for first in reversed(range(0, tokens, block)):
        keys = first + block
        bias = pair_bias(seg_col, seg_row, first, block, keys)
        queries = q_ref[first:keys, :]
        grads = g_ref[first:keys, :]
        dq = jnp.zeros((block, width), F)
        stacks = ([], [], [], [])
        for head in range(heads):
            q_head = queries * (masks[head] * SCORE_SCALE)
            g_head = grads * masks[head]
            scores = dotg(q_head, k_ref[:keys, :], NT) + bias
            probs = jnp.exp(scores - lse_ref[first:keys, head : head + 1])
            weighted = probs * dotg(g_head, v_ref[:keys, :], NT)
            delta = jnp.sum(weighted, axis=-1, keepdims=True)
            grad_scores = (weighted - probs * delta).astype(B)
            dq += jnp.dot(grad_scores, k_ref[:keys, :] * masks[head], preferred_element_type=F)
            for stack, value in zip(stacks, (grad_scores, q_head, probs.astype(B), g_head)):
                stack.append(value)
        joined = [jnp.concatenate(stack, 0) for stack in stacks]
        dk = dotg(joined[0], joined[1], TN)
        dv = dotg(joined[2], joined[3], TN)
        if keys == tokens:
            dk_ref[...] = dk
            dv_ref[...] = dv
        else:
            dk_ref[:keys, :] += dk
            dv_ref[:keys, :] += dv
        dq_ref[first:keys, :] = dq * SCORE_SCALE
    tables = (same_ref[...], ahead_ref[...], behind_ref[...])
    pieces = (unrotated(dq_ref[...], *tables), unrotated(dk_ref[...], *tables), dv_ref[...])
    for at, piece in enumerate(pieces):
        rounded = piece.astype(B)
        out_ref[:, at * width : (at + 1) * width] = rounded
        bias_ref[:, at * width : (at + 1) * width] = jnp.sum(
            rounded.astype(F), axis=0, keepdims=True
        )


def attend_back(q, k, v, grads, lse, seg_col, seg_row, tables, heads):
    tokens, width = q.shape
    return pl.pallas_call(
        functools.partial(attend_back_body, heads),
        out_shape=[
            jax.ShapeDtypeStruct((tokens, 3 * width), B),
            jax.ShapeDtypeStruct((1, 3 * width), F),
        ],
        scratch_shapes=[pltpu.VMEM((tokens, width), F)] * 3,
        name="attend_back",
    )(q, k, v, grads, lse, seg_col, seg_row, *tables)


def project_back_body(grad_ref, w_ref, x_ref, e_ref, sums_ref):
    hat, _ = unit_rows(x_ref[...].astype(F))
    e = dotg(grad_ref[...], w_ref[...], NT)
    e_ref[...] = e.astype(B)
    sums = jnp.concatenate(
        [jnp.sum(e * hat, axis=0, keepdims=True), jnp.sum(e, axis=0, keepdims=True)], 0
    )

    @pl.when(pl.program_id(0) == 0)
    def _():
        sums_ref[...] = sums

    @pl.when(pl.program_id(0) != 0)
    def _():
        sums_ref[...] += sums


def project_back(grad_proj, w_mine, x_all):
    tokens, features = x_all.shape
    block = min(TOKEN_BLOCK, tokens)
    return pl.pallas_call(
        project_back_body,
        grid=(tokens // block,),
        in_specs=[
            row_spec(grad_proj.shape[1], block),
            whole_spec(w_mine),
            row_spec(features, block),
        ],
        out_specs=[
            row_spec(features, block),
            pl.BlockSpec((2, features), lambda i: (0, 0)),
        ],
        out_shape=[
            jax.ShapeDtypeStruct((tokens, features), B),
            jax.ShapeDtypeStruct((2, features), F),
        ],
        name="project_back",
    )(grad_proj, w_mine, x_all)


def adam_step(parameter, gradient, moments):
    first_moment = BETA_ONE * moments[0] + (1.0 - BETA_ONE) * gradient
    second_moment = BETA_TWO * moments[1] + (1.0 - BETA_TWO) * gradient * gradient
    return first_moment / BIAS_FIRST / (
        jnp.sqrt(second_moment / BIAS_SECOND) + ADAM_EPS
    ) + DECAY_RATE * parameter.astype(F)


def rotary_tables(segment_row, width):
    tokens = segment_row.shape[0]
    before = jnp.sum((segment_row[None, :] < segment_row[:, None]).astype(jnp.int32), axis=1)
    positions = jnp.arange(tokens, dtype=jnp.int32) - before
    frequency = jnp.exp(
        jnp.arange(HALF_ROT, dtype=F) * (-2.0 * jnp.log(ROPE_BASE) / ROT_DIMS)
    )
    angles = positions.astype(F)[:, None] * frequency[None, :]
    cosine = jnp.cos(angles)
    sine = jnp.sin(angles)
    none = jnp.zeros((tokens, HALF_ROT), F)
    rest = jnp.zeros((tokens, HEAD_DIM - ROT_DIMS), F)
    heads = width // HEAD_DIM
    tile = lambda *parts: jnp.tile(jnp.concatenate(parts, 1), (1, heads))
    return (
        tile(cosine, cosine, rest + 1.0),
        tile(-sine, none, rest),
        tile(none, sine, rest),
    )


def packed_rows(parts, rows, columns):
    flat = jnp.concatenate(parts, -1)
    room = rows * columns - flat.shape[-1]
    flat = jnp.concatenate([flat, jnp.zeros(flat.shape[:-1] + (room,), flat.dtype)], -1)
    return flat.reshape(flat.shape[:-1] + (rows, columns))


def shards(
    block_input, out_grad, segment_ids, positions, norm_params, w_qkv, b_qkv, w_out, gate_up, w_down,
    moment_norm, moment_qkv, moment_bias, moment_out, moment_gate, moment_down,
):
    x_own = block_input[0]
    local_len, features = x_own.shape
    rows = lax.axis_size("rows")
    wide = lax.axis_size("wide")
    my_row = lax.axis_index("rows")
    my_wide = lax.axis_index("wide")
    segment_row = segment_ids[0]
    heads = HEADS // wide
    width = heads * HEAD_DIM
    depth = w_qkv.shape[0]
    norm_size = norm_params.shape[1]
    strided = depth % HEAD_DIM == 0

    def by_head(array, axis):
        shape = array.shape
        if strided:
            array = array.reshape(shape[:axis] + (heads, wide, HEAD_DIM) + shape[axis + 1 :])
            return jnp.moveaxis(array, axis + 1, 0)
        array = array.reshape(shape[:axis] + (wide, heads, HEAD_DIM) + shape[axis + 1 :])
        return jnp.moveaxis(array, axis, 0)

    def from_heads(array, axis):
        array = jnp.moveaxis(array, 0, axis + 1 if strided else axis)
        shape = array.shape
        return array.reshape(shape[:axis] + (HEADS * HEAD_DIM,) + shape[axis + 3 :])

    w_blocks = by_head(w_qkv.reshape(depth, 3, features), 2).reshape(wide, depth, 3 * width)
    extra = packed_rows([norm_params.reshape(-1), b_qkv], EXTRA_ROWS, 3 * width)
    w_blocks = jnp.concatenate(
        [w_blocks, jnp.broadcast_to(extra[None], (wide,) + extra.shape)], 1
    )
    w_packed = rows_gather(wide_exchange(w_blocks), 0)
    w_mine = w_packed[:, :depth].reshape(features, 3 * width)
    extra = w_packed[:, depth:].reshape(rows * wide, -1)
    norms = extra[:, : 4 * norm_size].reshape(rows * wide, 4, norm_size)
    norms = norms.transpose(1, 0, 2).reshape(4, features).astype(F)
    bias = extra[:, 4 * norm_size : 4 * norm_size + b_qkv.shape[0]].reshape(3, features)
    bias_mine = lax.dynamic_index_in_dim(by_head(bias, 1), my_wide, 0, False)
    bias_mine = bias_mine.reshape(1, 3 * width).astype(F)
    if strided:
        out_mine = rows_gather(w_out, 0)
    else:
        out_mine = lax.all_gather(w_out, ("rows", "wide"), axis=0, tiled=True)
        out_mine = lax.dynamic_slice_in_dim(out_mine, my_wide * width, width, 0)

    x_all = wide_gather(x_own)
    tables = rotary_tables(segment_row, width)
    seg_col = segment_row[:, None]
    seg_line = segment_row[None, :]
    q, k, v, normed_all = project(x_all, norms[:2], w_mine, bias_mine, tables)
    attended, lse = attend(q, k, v, seg_col, seg_line, heads)
    branch = jnp.dot(attended, out_mine, preferred_element_type=F).astype(B)
    after_attn = x_own.astype(F) + wide_scatter(branch)
    hat_two, inv_two = unit_rows(after_attn)
    normed_two = (hat_two * norms[2] + norms[3]).astype(B)
    tokens_all = wide_gather(normed_two)
    gate_rows = rows_gather(gate_up, 1)
    down_rows = rows_gather(w_down, 1)
    gate_vals = jnp.einsum("td,gdf->gtf", tokens_all, gate_rows, preferred_element_type=F)
    gate_part, up_part = gate_vals[0], gate_vals[1]
    sigmoid_g = jax.nn.sigmoid(gate_part)
    activated = gate_part * sigmoid_g
    hidden = (activated * up_part).astype(B)
    mlp_out = wide_scatter(jnp.dot(hidden, down_rows, preferred_element_type=F).astype(B))
    block_out = (after_attn + mlp_out).astype(B)

    grads_all = wide_gather(out_grad[0])
    grad_hidden = jnp.einsum("td,fd->tf", grads_all, down_rows, preferred_element_type=F)
    down_grad = jnp.einsum("tf,td->fd", hidden, grads_all, preferred_element_type=F).astype(B)
    grad_gate_part = grad_hidden * up_part * sigmoid_g * (1.0 + gate_part * (1.0 - sigmoid_g))
    gate_grads = jnp.stack([grad_gate_part, grad_hidden * activated]).astype(B)
    grad_normed_two = wide_scatter(
        jnp.einsum("gtf,gdf->td", gate_grads, gate_rows, preferred_element_type=F).astype(B)
    )
    gate_grad = jnp.einsum("td,gtf->gdf", tokens_all, gate_grads, preferred_element_type=F).astype(B)
    grad_gate = rows_scatter(gate_grad, 1)
    grad_down = rows_scatter(down_grad, 1)

    def norm_back(upstream, hat, inverse, gain):
        scaled = upstream * gain
        mean_grad = jnp.mean(scaled, axis=-1, keepdims=True)
        mean_proj = jnp.mean(scaled * hat, axis=-1, keepdims=True)
        return inverse * (scaled - mean_grad - hat * mean_proj)

    grad_after = out_grad[0].astype(F) + norm_back(grad_normed_two, hat_two, inv_two, norms[2])
    gain_two = jnp.sum(grad_normed_two * hat_two, axis=0)
    shift_two = jnp.sum(grad_normed_two, axis=0)
    branch_all = wide_gather(grad_after.astype(B))
    grad_attended = dotg(branch_all, out_mine, NT).astype(B)
    out_part = dotg(attended, branch_all, TN).astype(B)
    if strided:
        grad_out = rows_scatter(out_part, 0)
    else:
        grad_out = rows_scatter(out_part, 0)
        moves = [
            (r * wide + w, w * rows + r) for r in range(rows) for w in range(wide)
        ]
        grad_out = lax.ppermute(grad_out, ("rows", "wide"), moves)
    grad_proj, bias_grad = attend_back(
        q, k, v, grad_attended, lse, seg_col, seg_line, tables, heads
    )
    e_one, sums_one = project_back(grad_proj, w_mine, x_all)
    grad_normed_one = wide_scatter(e_one)
    qkv_part = dotg(normed_all, grad_proj, TN).astype(B)
    hat_one, inv_one = unit_rows(x_own.astype(F))
    input_grad = grad_after + norm_back(grad_normed_one, hat_one, inv_one, norms[0])

    norm_parts = jnp.concatenate([sums_one, gain_two[None], shift_two[None]], 0)
    norm_parts = norm_parts.reshape(4, rows * wide, norm_size).transpose(1, 0, 2)
    extra = packed_rows(
        [
            norm_parts.reshape(rows * wide, -1),
            jnp.broadcast_to(bias_grad, (rows * wide, 3 * width)),
        ],
        EXTRA_ROWS,
        3 * width,
    ).astype(B)
    packed = jnp.concatenate([qkv_part.reshape(rows * wide, depth, 3 * width), extra], 1)
    received = wide_exchange(rows_scatter(packed, 0).astype(B)).astype(F)
    grad_qkv = received[:, :depth].reshape(wide, depth, 3, heads, HEAD_DIM)
    grad_qkv = from_heads(grad_qkv, 2).reshape(depth, 3 * features)
    extra = received[:, depth:].reshape(wide, -1)
    grad_norms = jnp.sum(extra[:, : 4 * norm_size], axis=0).reshape(4, norm_size)
    bias_all = extra[:, 4 * norm_size : 4 * norm_size + 3 * width]
    bias_all = from_heads(bias_all.reshape(wide, 3, heads, HEAD_DIM), 1).reshape(-1)
    size = b_qkv.shape[0]
    grad_bias = lax.dynamic_slice_in_dim(bias_all, (my_row * wide + my_wide) * size, size, 0)

    return (
        block_out[None],
        input_grad[None],
        grad_norms,
        grad_qkv,
        grad_bias,
        grad_out,
        grad_gate,
        grad_down,
        adam_step(norm_params, grad_norms, moment_norm),
        adam_step(w_qkv, grad_qkv, moment_qkv),
        adam_step(b_qkv, grad_bias, moment_bias),
        adam_step(w_out, grad_out, moment_out),
        adam_step(gate_up, grad_gate, moment_gate),
        adam_step(w_down, grad_down, moment_down),
    )


def solution(mesh):
    both = ("rows", "wide")
    tokens = P("rows", "wide", None)
    weights = (P(None, both), P(both, None), P(both), P(both, None), P(None, "rows", "wide"), P("wide", "rows"))
    moments = tuple(P(None, *spec) for spec in weights)
    return jax.shard_map(
        shards,
        mesh=mesh,
        in_specs=(tokens, tokens, P("rows", None), P("rows", "wide")) + weights + moments,
        out_specs=(tokens, tokens) + weights + weights,
        check_vma=False,
    )
```

```python
import functools
import math

import jax
import jax.numpy as jnp
from jax import lax
from jax.experimental import pallas as pl
from jax.experimental.pallas import tpu as pltpu
from jax.sharding import PartitionSpec as P

F = jnp.float32
B = jnp.bfloat16
HEADS = 32
HEAD_DIM = 64
ROT_DIMS = 16
HALF_ROT = ROT_DIMS // 2
NORM_EPS = 1e-05
NEG_LARGE = -1e30
SCORE_SCALE = 0.125
ROPE_BASE = 10000.0
BETA_ONE = 0.9
BETA_TWO = 0.95
BIAS_FIRST = 0.999973438601112
BIAS_SECOND = 0.994079470779667
ADAM_EPS = 1e-08
DECAY_RATE = 0.1
TOKEN_BLOCK = 256
EXTRA_ROWS = 8
NT = (((1,), (1,)), ((), ()))
TN = (((0,), (0,)), ((), ()))


def dotg(left, right, dims):
    return lax.dot_general(left, right, dims, preferred_element_type=F)


def plus(left, right):
    return (left.astype(F) + right.astype(F)).astype(B)


def rows_swap(value, bits):
    return lax.ppermute(value, "rows", [(i, i ^ bits) for i in range(4)])


class RowsGather:
    def __init__(self, shard, axis):
        self.axis = axis
        self.size = shard.shape[axis]
        self.step = self.whole = None
        if lax.axis_size("rows") == 4:
            self.shard = shard
            self.step = (rows_swap(shard, 1), rows_swap(shard, 2))
        else:
            self.whole = lax.all_gather(shard, "rows", axis=axis, tiled=True)

    def before(self, *values):
        if self.step is not None:
            near, far, *values = tie(*self.step, *values)
            self.step = (near, far)
        return values if len(values) > 1 else values[0]

    def second(self):
        if self.step is not None:
            self.near, self.far = self.step
            half = self.size // 2
            first = lax.slice_in_dim(self.near, 0, half, axis=self.axis)
            last = lax.slice_in_dim(self.far, half, self.size, axis=self.axis)
            self.step = (rows_swap(first, 2), rows_swap(last, 1))
        return self

    def pieces(self):
        if self.whole is not None:
            return [self.whole], [jnp.int32(0)]
        me = lax.axis_index("rows")
        places = [(me ^ bits) * self.size for bits in range(4)]
        arrays = [self.shard, self.near, self.far, *self.step]
        return arrays, places + [places[3] + self.size // 2]

    def join(self):
        if self.whole is not None:
            return self.whole
        shape = list(self.shard.shape)
        shape[self.axis] = 4 * self.size
        whole = jnp.zeros(shape, self.shard.dtype)
        for piece, place in zip(*self.pieces()):
            whole = lax.dynamic_update_slice_in_dim(whole, piece, place, self.axis)
        return whole


class RowsSum:
    def __init__(self, whole, axis):
        self.whole, self.axis = whole, axis
        self.arrived = self.sent = None
        if lax.axis_size("rows") == 4:
            diagonal = self.part(3)
            half = diagonal.shape[0] // 2
            self.arrived = (rows_swap(diagonal[:half], 1), rows_swap(diagonal[half:], 2))

    def part(self, bits):
        size = self.whole.shape[self.axis] // 4
        start = (lax.axis_index("rows") ^ bits) * size
        return lax.dynamic_slice_in_dim(self.whole, start, size, self.axis)

    def before(self, value):
        if self.arrived is not None:
            near, far, value = tie(*self.arrived, value)
            self.arrived = (near, far)
        return value

    def result(self):
        if self.arrived is None:
            return lax.psum_scatter(
                self.whole, "rows", scatter_dimension=self.axis, tiled=True
            ).astype(F)
        if self.sent is None:
            self.second()
        far, near = self.sent
        return self.part(0).astype(F) + far.astype(F) + near.astype(F)

    def arrived_or_whole(self):
        return (self.whole,) if self.arrived is None else self.arrived

    def second(self):
        if self.arrived is None:
            return self.whole, self.whole
        near, far = self.part(1), self.part(2)
        half = near.shape[0] // 2
        far = jnp.concatenate([plus(far[:half], self.arrived[0]), far[half:]], 0)
        near = jnp.concatenate([near[:half], plus(near[half:], self.arrived[1])], 0)
        self.sent = (rows_swap(far, 2), rows_swap(near, 1))
        return far, near

    def after(self, *values):
        if self.arrived is None:
            self.whole, *values = tie(self.whole, *values)
        else:
            far, near, *values = tie(*self.sent, *values)
            self.sent = (far, near)
        return values if len(values) > 1 else values[0]


def wide_exchange(blocks, between=None):
    count = lax.axis_size("wide")
    me = lax.axis_index("wide")
    whole = jnp.zeros(blocks.shape, blocks.dtype)
    moved = []
    for step in range(count):
        block = lax.dynamic_slice_in_dim(blocks, (me + step) % count, 1, 0)
        if step:
            block = lax.ppermute(block, "wide", [(i, (i + step) % count) for i in range(count)])
        moved.append(block)
    values = ()
    if between is not None:
        half = count // 2
        moved[half:], values = split_tie(moved[half:], between(moved[:half]))
    for step, block in enumerate(moved):
        whole = lax.dynamic_update_slice_in_dim(whole, block, (me - step) % count, 0)
    return whole, values


def wide_gather(shard):
    return lax.all_gather(shard, "wide", axis=0, tiled=True)


def wide_scatter(whole):
    return lax.psum_scatter(whole, "wide", scatter_dimension=0, tiled=True)


def tie(*values):
    return lax.optimization_barrier(values)


def split_tie(first, second):
    values = list(tie(*first, *second))
    return values[: len(first)], values[len(first) :]


def chip_pairs(move):
    pairs = []
    for at in range(lax.axis_size("wide")):
        target = move(at // 2, at % 2)
        if target is not None:
            pairs.append((at, target[0] * 2 + target[1]))
    return pairs


def core_swap(value):
    return lax.ppermute(value, "wide", chip_pairs(lambda chip, core: (chip, 1 - core)))


def line_step(right, left, step, spread):
    chips = lax.axis_size("wide") // 2

    def sends(passed):
        return step <= passed if spread else passed <= step

    right = lax.ppermute(
        right,
        "wide",
        chip_pairs(
            lambda chip, core: (chip + 1, core) if chip < chips - 1 and sends(chip) else None
        ),
    )
    left = lax.ppermute(
        left,
        "wide",
        chip_pairs(
            lambda chip, core: (chip - 1, core) if 0 < chip and sends(chips - 1 - chip) else None
        ),
    )
    return right, left


class LineSum:
    def __init__(self, whole):
        self.chips = lax.axis_size("wide") // 2
        at = lax.axis_index("wide")
        self.chip, core = at // 2, at % 2
        size = whole.shape[0] // (2 * self.chips)
        parts = whole.reshape((self.chips, 2, size) + whole.shape[1:])
        mine = lax.dynamic_index_in_dim(parts, core, 1, False)
        swapped = core_swap(lax.dynamic_index_in_dim(parts, 1 - core, 1, False))
        self.parts = plus(mine, swapped)
        self.flows = None
        self.step = 0

    def part(self, chip):
        return lax.dynamic_index_in_dim(self.parts, jnp.clip(chip, 0, self.chips - 1), 0, False)

    def prepare(self):
        to_right = self.part(self.chips - 1 - self.step + self.chip)
        to_left = self.part(self.step - (self.chips - 1 - self.chip))
        if self.flows is not None:
            to_right = plus(to_right, self.flows[0])
            to_left = plus(to_left, self.flows[1])
        self.flows = (to_right, to_left)

    def advance(self):
        self.flows = line_step(*self.flows, self.step, False)
        self.step += 1

    def before(self, value):
        right, left, value = tie(*self.flows, value)
        self.flows = (right, left)
        return value

    def result(self):
        while self.step < self.chips - 1:
            self.prepare()
            self.advance()
        return self.part(self.chip).astype(F) + self.flows[0].astype(F) + self.flows[1].astype(F)


def rotated(value, same, ahead, behind):
    width = value.shape[1]
    return (
        value * same
        + pltpu.roll(value, width - HALF_ROT, 1) * ahead
        + pltpu.roll(value, HALF_ROT, 1) * behind
    )


def unrotated(value, same, ahead, behind):
    width = value.shape[1]
    return value * same - (
        pltpu.roll(value, width - HALF_ROT, 1) * ahead
        + pltpu.roll(value, HALF_ROT, 1) * behind
    )


def wide_tables(width, *refs):
    return [jnp.concatenate([ref[...]] * (width // ref.shape[1]), 1) for ref in refs]


def tables_body(col_ref, row_ref, same_ref, ahead_ref, behind_ref):
    tokens, lanes = same_ref.shape
    col = col_ref[...]
    before = jnp.zeros((tokens, 1), jnp.int32)
    for first in range(0, tokens, TOKEN_BLOCK):
        smaller = row_ref[:, first : first + TOKEN_BLOCK] < col
        before += jnp.sum(jnp.where(smaller, 1, 0), axis=1, keepdims=True)
    positions = lax.broadcasted_iota(jnp.int32, (tokens, 1), 0) - before
    dim = lax.broadcasted_iota(jnp.int32, (1, lanes), 1) % HEAD_DIM
    frequency = jnp.exp((dim % HALF_ROT).astype(F) * (-2.0 * math.log(ROPE_BASE) / ROT_DIMS))
    angles = positions.astype(F) * frequency
    cosine, sine = jnp.cos(angles), jnp.sin(angles)
    same_ref[...] = jnp.where(dim < ROT_DIMS, cosine, 1.0)
    ahead_ref[...] = jnp.where(dim < HALF_ROT, -sine, 0.0)
    behind_ref[...] = jnp.where((dim >= HALF_ROT) & (dim < ROT_DIMS), sine, 0.0)


def rotary_tables(seg_col, seg_line):
    tokens = seg_col.shape[0]
    return pl.pallas_call(
        tables_body,
        out_shape=[jax.ShapeDtypeStruct((tokens, 2 * HEAD_DIM), F)] * 3,
        name="tables",
    )(seg_col, seg_line)


def unit_rows(tensor):
    center = tensor - jnp.mean(tensor, axis=-1, keepdims=True)
    inverse = lax.rsqrt(jnp.mean(center * center, axis=-1, keepdims=True) + NORM_EPS)
    return center * inverse, inverse


def cost(products, values):
    return pl.CostEstimate(flops=2 * products, transcendentals=0, bytes_accessed=values)


def project_body(pieces, depth, norm_size, *refs):
    place_ref, x_ref, same_ref, ahead_ref, behind_ref = refs[:5]
    w_refs = refs[5 : 5 + pieces]
    q_ref, k_ref, v_ref, hat_ref, w_ref, norms_ref, bias_ref = refs[5 + pieces :]

    @pl.when(pl.program_id(0) == 0)
    def _():
        bias_ref[...] = jnp.zeros_like(bias_ref)
        for at, piece in enumerate(w_refs):
            blocks = piece.shape[0]
            rows = pl.multiple_of(place_ref[at] * depth, blocks * depth)
            columns = pl.multiple_of(place_ref[at] * norm_size, blocks * norm_size)
            for block in range(blocks):
                w_ref[pl.ds(rows + block * depth, depth), :] = piece[block, :depth]
                bias_ref[...] += piece[block, depth + 4 : depth + 5].astype(F)
            norms = [piece[block, depth : depth + 4, :norm_size].astype(F) for block in range(blocks)]
            norms_ref[:, pl.ds(columns, blocks * norm_size)] = jnp.concatenate(norms, 1)

    hat, _ = unit_rows(x_ref[...].astype(F))
    normed = (hat * norms_ref[0:1, :] + norms_ref[1:2, :]).astype(B)
    hat_ref[...] = hat.astype(B)
    out = jnp.dot(normed, w_ref[...], preferred_element_type=F) + bias_ref[...]
    width = q_ref.shape[1]
    tables = wide_tables(width, same_ref, ahead_ref, behind_ref)
    q_ref[...] = rotated(out[:, :width], *tables).astype(B)
    k_ref[...] = rotated(out[:, width : 2 * width], *tables).astype(B)
    v_ref[...] = out[:, 2 * width :].astype(B)


def row_spec(width, block):
    return pl.BlockSpec((block, width), lambda i: (i, 0))


def whole_spec(array):
    return pl.BlockSpec(array.shape, lambda i: (0, 0))


def project(x_all, gathered, tables, depth, norm_size):
    tokens, features = x_all.shape
    pieces, places = gathered.pieces()
    columns = pieces[0].shape[2]
    width = columns // 3
    block = min(TOKEN_BLOCK, tokens)
    row = lambda size: pl.BlockSpec((block, size), lambda i, place: (i, 0))
    flat = lambda *shape: pl.BlockSpec(shape, lambda i, place: (0,) * len(shape))
    return pl.pallas_call(
        functools.partial(project_body, len(pieces), depth, norm_size),
        grid_spec=pltpu.PrefetchScalarGridSpec(
            num_scalar_prefetch=1,
            grid=(tokens // block,),
            in_specs=[row(features)]
            + [row(table.shape[1]) for table in tables]
            + [flat(*piece.shape) for piece in pieces],
            out_specs=[row(width)] * 3
            + [row(features), flat(features, columns), flat(4, features), flat(1, columns)],
        ),
        out_shape=[jax.ShapeDtypeStruct((tokens, width), B)] * 3
        + [
            jax.ShapeDtypeStruct((tokens, features), B),
            jax.ShapeDtypeStruct((features, columns), B),
            jax.ShapeDtypeStruct((4, features), F),
            jax.ShapeDtypeStruct((1, columns), F),
        ],
        name="project",
        cost_estimate=cost(tokens * features * columns, 4 * tokens * features),
    )(jnp.stack(places), x_all, *tables, *pieces)


def gate_body(pieces, *refs):
    place_ref, tokens_ref = refs[:2]
    gate_ref, up_ref, hidden_ref = refs[2 + 2 * pieces :]
    sums = []
    for half in range(2):
        total = jnp.zeros(gate_ref.shape, F)
        for at in range(pieces):
            w_ref = refs[2 + half * pieces + at]
            size = w_ref.shape[1]
            columns = pl.ds(pl.multiple_of(place_ref[at], size), size)
            total += dotg(tokens_ref[:, columns], w_ref[...], NT)
        sums.append(total)
    gate_ref[...] = sums[0]
    up_ref[...] = sums[1]
    hidden_ref[...] = (sums[0] * jax.nn.sigmoid(sums[0]) * sums[1]).astype(B)


def piece_call(body, name, places, blocked, pieces, outs, products):
    tokens = blocked[0].shape[0]
    block = min(TOKEN_BLOCK, tokens)

    def spec(shape):
        if len(shape) == 3:
            return pl.BlockSpec((shape[0], block, shape[2]), lambda i, place: (0, i, 0))
        return pl.BlockSpec((block, shape[1]), lambda i, place: (i, 0))

    size = sum(array.size * array.dtype.itemsize for array in blocked + pieces)
    return pl.pallas_call(
        functools.partial(body, len(places)),
        grid_spec=pltpu.PrefetchScalarGridSpec(
            num_scalar_prefetch=1,
            grid=(tokens // block,),
            in_specs=[spec(array.shape) for array in blocked]
            + [pl.BlockSpec(piece.shape, lambda i, place: (0, 0)) for piece in pieces],
            out_specs=[spec(out.shape) for out in outs],
        ),
        out_shape=outs,
        name=name,
        cost_estimate=cost(products, size),
    )(jnp.stack(places), *blocked, *pieces)


def gate_up_forward(tokens_all, gate, up):
    tokens = tokens_all.shape[0]
    gates, places = gate.pieces()
    ups, _ = up.pieces()
    units = gates[0].shape[0]
    outs = [jax.ShapeDtypeStruct((tokens, units), kind) for kind in (F, F, B)]
    products = 2 * tokens * units * tokens_all.shape[1]
    return piece_call(gate_body, "gate_up", places, [tokens_all], gates + ups, outs, products)


def down_body(pieces, *refs):
    place_ref, hidden_ref = refs[:2]
    out_ref = refs[2 + pieces]
    for at in range(pieces):
        w_ref = refs[2 + at]
        size = w_ref.shape[1]
        columns = pl.ds(pl.multiple_of(place_ref[at], size), size)
        out_ref[:, columns] = jnp.dot(
            hidden_ref[...], w_ref[...], preferred_element_type=F
        ).astype(B)


def down_forward(hidden, down, features):
    tokens, units = hidden.shape
    downs, places = down.pieces()
    outs = [jax.ShapeDtypeStruct((tokens, features), B)]
    return piece_call(
        down_body, "down", places, [hidden], downs, outs, tokens * units * features
    )[0]


def feed_back_body(pieces, *refs):
    place_ref, grads_ref, gate_ref, up_ref = refs[:4]
    weights = refs[4 : 4 + 3 * pieces]
    out_ref, e_ref = refs[4 + 3 * pieces :]
    grad_hidden = jnp.zeros(gate_ref.shape, F)
    for at in range(pieces):
        size = weights[at].shape[1]
        columns = pl.ds(pl.multiple_of(place_ref[at], size), size)
        grad_hidden += dotg(grads_ref[:, columns], weights[at][...], NT)
    gate = gate_ref[...]
    sigmoid = jax.nn.sigmoid(gate)
    grad_gate = grad_hidden * up_ref[...] * sigmoid * (1.0 + gate * (1.0 - sigmoid))
    grad_gate = grad_gate.astype(B)
    grad_up = (grad_hidden * (gate * sigmoid)).astype(B)
    out_ref[0] = grad_gate
    out_ref[1] = grad_up
    for at in range(pieces):
        size = weights[at].shape[1]
        columns = pl.ds(pl.multiple_of(place_ref[at], size), size)
        e = jnp.dot(grad_gate, weights[pieces + at][...], preferred_element_type=F)
        e += jnp.dot(grad_up, weights[2 * pieces + at][...], preferred_element_type=F)
        e_ref[:, columns] = e.astype(B)


def feed_back(grads_all, gate_part, up_part, down, gate, up):
    tokens, features = grads_all.shape
    units = gate_part.shape[1]
    downs, places = down.pieces()
    outs = [
        jax.ShapeDtypeStruct((2, tokens, units), B),
        jax.ShapeDtypeStruct((tokens, features), B),
    ]
    weights = downs + gate.pieces()[0] + up.pieces()[0]
    return piece_call(
        feed_back_body,
        "feed_back",
        places,
        [grads_all, gate_part, up_part],
        weights,
        outs,
        3 * tokens * units * features,
    )


def pair_bias(seg_col, seg_row, first, size, keys):
    same = seg_col[first : first + size, :] == seg_row[:, :keys]
    key_pos = lax.broadcasted_iota(jnp.int32, (size, keys), 1)
    query_pos = first + lax.broadcasted_iota(jnp.int32, (size, keys), 0)
    return jnp.where(same & (key_pos <= query_pos), 0.0, NEG_LARGE)


def head_masks(heads, width):
    lane = lax.broadcasted_iota(jnp.int32, (1, width), 1) // HEAD_DIM
    return [jnp.where(lane == head, 1.0, 0.0).astype(B) for head in range(heads)]


def attend_body(heads, q_ref, k_ref, v_ref, seg_col, seg_row, out_ref, lse_ref):
    tokens, width = q_ref.shape
    block = min(TOKEN_BLOCK, tokens)
    masks = head_masks(heads, width)
    for first in range(0, tokens, block):
        keys = first + block
        bias = pair_bias(seg_col, seg_row, first, block, keys)
        queries = q_ref[first:keys, :]
        total = jnp.zeros((block, width), F)
        for head in range(heads):
            scores = dotg(queries * (masks[head] * SCORE_SCALE), k_ref[:keys, :], NT) + bias
            top = jnp.max(scores, axis=-1, keepdims=True)
            weights = jnp.exp(scores - top)
            norm = jnp.sum(weights, axis=-1, keepdims=True)
            probs = (weights * (1.0 / norm)).astype(B)
            total += jnp.dot(probs, v_ref[:keys, :] * masks[head], preferred_element_type=F)
            lse_ref[first:keys, head : head + 1] = top + jnp.log(norm)
        out_ref[first:keys, :] = total.astype(B)


def attend(q, k, v, seg_col, seg_row, heads):
    tokens, width = q.shape
    return pl.pallas_call(
        functools.partial(attend_body, heads),
        out_shape=[
            jax.ShapeDtypeStruct((tokens, width), B),
            jax.ShapeDtypeStruct((tokens, 128), F),
        ],
        name="attend",
        cost_estimate=cost(heads * tokens * tokens * 512, 8 * tokens * width),
    )(q, k, v, seg_col, seg_row)


def out_project_body(
    core_ref, attended_ref, same_ref, other_ref, x_ref, norm_ref, normed_ref, after_ref
):
    core = core_ref[0]
    width = attended_ref.shape[2]
    total = x_ref[...].astype(F)
    for chip in range(same_ref.shape[1]):
        for w_ref, which in ((same_ref, core), (other_ref, 1 - core)):
            weights = w_ref[:, chip].reshape(width, w_ref.shape[3])
            total += jnp.dot(attended_ref[chip * 2 + which], weights, preferred_element_type=F)
    after_ref[...] = total
    hat, _ = unit_rows(total)
    normed_ref[...] = (hat * norm_ref[0:1, :] + norm_ref[1:2, :]).astype(B)


def out_project(core, attended_all, out_same, out_other, x_all, norm_two):
    owners, tokens, width = attended_all.shape
    features = x_all.shape[1]
    block = min(TOKEN_BLOCK, tokens)
    weights = pl.BlockSpec(out_same.shape, lambda i, core: (0, 0, 0, 0))
    rows = pl.BlockSpec((block, features), lambda i, core: (i, 0))
    return pl.pallas_call(
        out_project_body,
        grid_spec=pltpu.PrefetchScalarGridSpec(
            num_scalar_prefetch=1,
            grid=(tokens // block,),
            in_specs=[
                pl.BlockSpec((owners, block, width), lambda i, core: (0, i, 0)),
                weights,
                weights,
                rows,
                pl.BlockSpec(norm_two.shape, lambda i, core: (0, 0)),
            ],
            out_specs=[rows, rows],
        ),
        out_shape=[
            jax.ShapeDtypeStruct((tokens, features), B),
            jax.ShapeDtypeStruct((tokens, features), F),
        ],
        name="out_project",
        cost_estimate=cost(tokens * features * features, 8 * tokens * features),
    )(core, attended_all, out_same, out_other, x_all, norm_two)


def attend_back_body(
    heads, q_ref, k_ref, v_ref, g_ref, lse_ref, seg_col, seg_row, same_ref, ahead_ref, behind_ref,
    out_ref, bias_ref, dq_ref, dk_ref, dv_ref,
):
    tokens, width = q_ref.shape
    block = min(TOKEN_BLOCK, tokens)
    masks = head_masks(heads, width)
    for first in reversed(range(0, tokens, block)):
        keys = first + block
        bias = pair_bias(seg_col, seg_row, first, block, keys)
        queries = q_ref[first:keys, :]
        grads = g_ref[first:keys, :]
        dq = jnp.zeros((block, width), F)
        stacks = ([], [], [], [])
        for head in range(heads):
            q_head = queries * (masks[head] * SCORE_SCALE)
            g_head = grads * masks[head]
            scores = dotg(q_head, k_ref[:keys, :], NT) + bias
            probs = jnp.exp(scores - lse_ref[first:keys, head : head + 1])
            weighted = probs * dotg(g_head, v_ref[:keys, :], NT)
            delta = jnp.sum(weighted, axis=-1, keepdims=True)
            grad_scores = (weighted - probs * delta).astype(B)
            dq += jnp.dot(grad_scores, k_ref[:keys, :] * masks[head], preferred_element_type=F)
            for stack, value in zip(stacks, (grad_scores, q_head, probs.astype(B), g_head)):
                stack.append(value)
        joined = [jnp.concatenate(stack, 0) for stack in stacks]
        dk = dotg(joined[0], joined[1], TN)
        dv = dotg(joined[2], joined[3], TN)
        if keys == tokens:
            dk_ref[...] = dk
            dv_ref[...] = dv
        else:
            dk_ref[:keys, :] += dk
            dv_ref[:keys, :] += dv
        dq_ref[first:keys, :] = dq * SCORE_SCALE
    tables = wide_tables(width, same_ref, ahead_ref, behind_ref)
    pieces = (unrotated(dq_ref[...], *tables), unrotated(dk_ref[...], *tables), dv_ref[...])
    for at, piece in enumerate(pieces):
        rounded = piece.astype(B)
        out_ref[:, at * width : (at + 1) * width] = rounded
        bias_ref[:, at * width : (at + 1) * width] = jnp.sum(
            rounded.astype(F), axis=0, keepdims=True
        )


def attend_back(q, k, v, grads, lse, seg_col, seg_row, tables, heads):
    tokens, width = q.shape
    return pl.pallas_call(
        functools.partial(attend_back_body, heads),
        out_shape=[
            jax.ShapeDtypeStruct((tokens, 3 * width), B),
            jax.ShapeDtypeStruct((1, 3 * width), F),
        ],
        scratch_shapes=[pltpu.VMEM((tokens, width), F)] * 3,
        name="attend_back",
        cost_estimate=cost(heads * tokens * tokens * 1024, 16 * tokens * width),
    )(q, k, v, grads, lse, seg_col, seg_row, *tables)


def weights_back_body(
    depth, norm_size, hat_ref, grad_ref, w_ref, norms_ref, two_ref, bias_ref, out_ref
):
    blocks, rows, columns = out_ref.shape
    product = dotg(hat_ref[...], grad_ref[...], TN)
    weights = w_ref[...].astype(F)
    bias = bias_ref[...]
    gain = jnp.sum(product * weights, axis=1, keepdims=True)
    shift = jnp.sum(weights * bias, axis=1, keepdims=True)
    lanes = lax.broadcasted_iota(jnp.int32, (gain.shape[0], 128), 1)
    ones = jnp.where(lanes == 0, gain, shift).T
    norms = jnp.concatenate([norms_ref[...]] * 2, 0).T
    product = (product * norms[:, 0:1] + norms[:, 1:2] * bias).astype(B)
    sums = jnp.concatenate([ones[:2], two_ref[...]], 0).astype(B)
    bias = bias.astype(B)
    for block in range(blocks):
        out_ref[block, :depth, :] = product[block * depth : (block + 1) * depth]
        mine = sums[:, block * norm_size : (block + 1) * norm_size]
        out_ref[block, depth:, :] = jnp.concatenate(
            [
                jnp.concatenate([mine, jnp.zeros((4, columns - norm_size), B)], 1),
                bias,
                jnp.zeros((rows - depth - 5, columns), B),
            ],
            0,
        )


def weights_back(hat_all, grad_proj, w_mine, norms, two, bias_grad, depth, norm_size):
    tokens, features = hat_all.shape
    columns = grad_proj.shape[1]
    block = min(256, features)
    flat = lambda array: pl.BlockSpec(array.shape, lambda i: (0, 0))
    across = lambda rows: pl.BlockSpec((rows, block), lambda i: (0, i))
    return pl.pallas_call(
        functools.partial(weights_back_body, depth, norm_size),
        grid=(features // block,),
        in_specs=[
            across(tokens),
            flat(grad_proj),
            row_spec(columns, block),
            across(4),
            across(2),
            flat(bias_grad),
        ],
        out_specs=pl.BlockSpec((block // depth, depth + EXTRA_ROWS, columns), lambda i: (i, 0, 0)),
        out_shape=jax.ShapeDtypeStruct((features // depth, depth + EXTRA_ROWS, columns), B),
        name="weights_back",
        cost_estimate=cost(tokens * features * columns, 4 * tokens * features),
    )(hat_all, grad_proj, w_mine, norms, two, bias_grad)


def norm_back_body(e_ref, x_ref, upstream_ref, gain_ref, grad_ref, *refs):
    hat, inverse = unit_rows(x_ref[...].astype(F))
    e = e_ref[...].astype(F)
    scaled = e * gain_ref[...]
    mean_grad = jnp.mean(scaled, axis=-1, keepdims=True)
    mean_proj = jnp.mean(scaled * hat, axis=-1, keepdims=True)
    grad = upstream_ref[...].astype(F) + inverse * (scaled - mean_grad - hat * mean_proj)
    grad_ref[...] = grad
    if refs:
        rounded_ref, sums_ref = refs
        rounded_ref[...] = grad.astype(B)
        sums_ref[...] = jnp.concatenate(
            [jnp.sum(e * hat, axis=0, keepdims=True), jnp.sum(e, axis=0, keepdims=True)], 0
        )


def norm_back(e, x, upstream, gain, more):
    tokens, features = x.shape
    outs = [jax.ShapeDtypeStruct((tokens, features), F)]
    if more:
        outs += [jax.ShapeDtypeStruct((tokens, features), B), jax.ShapeDtypeStruct((2, features), F)]
    return pl.pallas_call(norm_back_body, out_shape=outs, name="norm_back")(e, x, upstream, gain)


def pack_body(strided, me_ref, w_ref, norm_ref, bias_ref, out_ref):
    wide, _, columns = out_ref.shape
    depth = w_ref.shape[0]
    third = w_ref.shape[1] // 3
    width = columns // 3
    me = me_ref[0]
    held = bias_ref.shape[1]
    padded = jnp.concatenate(
        [norm_ref[...], jnp.zeros((4, columns - norm_ref.shape[1]), B)], 1
    )
    for owner in range(wide):
        biases = []
        for part in range(3):
            for slot in range(width // HEAD_DIM):
                head = slot * wide + owner if strided else owner * (width // HEAD_DIM) + slot
                first = part * third + head * HEAD_DIM
                if slot % 2 == 0:
                    left = w_ref[:, first : first + HEAD_DIM]
                else:
                    to = part * width + (slot - 1) * HEAD_DIM
                    out_ref[owner, :depth, to : to + 2 * HEAD_DIM] = jnp.concatenate(
                        [left, w_ref[:, first : first + HEAD_DIM]], 1
                    )
                last = first + HEAD_DIM
                while first < last:
                    stop = min(last, (first // held + 1) * held)
                    mine = bias_ref[:, first % held : first % held + stop - first]
                    kept = jnp.where(me == first // held, mine.astype(F), 0.0)
                    biases.append(kept.astype(B))
                    first = stop
        out_ref[owner, depth:, :] = jnp.concatenate(
            [padded, jnp.concatenate(biases, 1), jnp.zeros((EXTRA_ROWS - 5, columns), B)], 0
        )


def pack(me, w_qkv, norm_params, b_qkv, strided, wide):
    depth, columns = w_qkv.shape
    memory = [pltpu.SMEM] + [pltpu.VMEM] * 3
    return pl.pallas_call(
        functools.partial(pack_body, strided),
        in_specs=[pl.BlockSpec(memory_space=space) for space in memory],
        out_shape=jax.ShapeDtypeStruct((wide, depth + EXTRA_ROWS, columns // wide), B),
        name="pack",
    )(me[None].astype(jnp.int32), w_qkv, norm_params, b_qkv[None])


def adam_step(parameter, gradient, moments):
    first_moment = BETA_ONE * moments[0] + (1.0 - BETA_ONE) * gradient
    second_moment = BETA_TWO * moments[1] + (1.0 - BETA_TWO) * gradient * gradient
    return first_moment / BIAS_FIRST / (
        jnp.sqrt(second_moment / BIAS_SECOND) + ADAM_EPS
    ) + DECAY_RATE * parameter.astype(F)


def finish_body(strided, wide, got_ref, w_ref, moment_ref, grad_ref, step_ref):
    depth = w_ref.shape[0]
    third = w_ref.shape[1] // 3
    width = got_ref.shape[2] // 3
    for part in range(3):
        for at in range(third // 128):
            if strided:
                slot, owner = at * 2 // wide, at * 2 % wide
                first = part * width + slot * HEAD_DIM
                gradient = jnp.concatenate(
                    [got_ref[owner + k, :depth, first : first + HEAD_DIM] for k in range(2)], 1
                )
            else:
                owner, first = at * 128 // width, part * width + at * 128 % width
                gradient = got_ref[owner, :depth, first : first + 128]
            gradient = gradient.astype(F)
            columns = slice(part * third + at * 128, part * third + at * 128 + 128)
            grad_ref[:, columns] = gradient
            step_ref[:, columns] = adam_step(
                w_ref[:, columns], gradient, (moment_ref[0, :, columns], moment_ref[1, :, columns])
            )


def finish(received, w_qkv, moments, strided):
    return pl.pallas_call(
        functools.partial(finish_body, strided, received.shape[0]),
        out_shape=[jax.ShapeDtypeStruct(w_qkv.shape, F)] * 2,
        name="finish",
    )(received, w_qkv, moments)


def shards(
    block_input, out_grad, segment_ids, positions, norm_params, w_qkv, b_qkv, w_out, gate_up, w_down,
    moment_norm, moment_qkv, moment_bias, moment_out, moment_gate, moment_down,
):
    x_own = block_input[0]
    local_len, features = x_own.shape
    rows = lax.axis_size("rows")
    wide = lax.axis_size("wide")
    my_row = lax.axis_index("rows")
    my_wide = lax.axis_index("wide")
    segment_row = segment_ids[0]
    heads = HEADS // wide
    width = heads * HEAD_DIM
    depth = w_qkv.shape[0]
    norm_size = norm_params.shape[1]
    strided = depth == HEAD_DIM

    bias_size = b_qkv.shape[0]
    chips = wide // 2
    core = my_wide % 2
    blocks = range(rows * wide)
    back = [(b % rows * wide + b // rows, b) for b in blocks]
    received, _ = wide_exchange(
        pack(my_row * wide + my_wide, w_qkv, norm_params, b_qkv, strided, wide)
    )
    received, x_first, segment_row = tie(received, x_own, segment_row)
    x_all = wide_gather(x_first)
    w_rows = RowsGather(received, 0)
    seg_col = segment_row[:, None]
    seg_line = segment_row[None, :]
    tables = w_rows.before(*rotary_tables(seg_col, seg_line))
    w_rows.second()
    gate_first = w_rows.before(gate_up.swapaxes(1, 2))
    gate = RowsGather(gate_first[0], 1)
    if strided:
        x_all, out_first = w_rows.before(x_all, w_out)
        out_line = lax.all_gather(out_first, "wide", axis=0, tiled=False)
    q, k, v, hat_all, w_mine, norms, _ = project(x_all, w_rows, tables, depth, norm_size)
    up = RowsGather(gate_first[1], 1)
    attended, lse = attend(q, k, v, seg_col, seg_line, heads)
    attended = gate.before(up.before(attended))
    if strided:
        attended, out_line = tie(attended, out_line)
    attended_all = lax.all_gather(attended, "wide", axis=0, tiled=False)
    if strided:
        out_line = out_line.reshape(chips, 2, depth, features)
        out_line = lax.dynamic_index_in_dim(out_line, core, 1, False)
        out_rows = RowsGather(out_line.reshape(chips * depth, features), 0)
        out_rows.second()
        out_rows.step = gate.before(*out_rows.step)
        out_rows.step = up.before(*out_rows.step)
        out_same = out_rows.join()
        out_other = core_swap(out_same)
        shape = (rows, chips, depth, features)
    else:
        shape = (1, chips, width, features)
        out_all = lax.all_gather(w_out, ("rows", "wide"), axis=0, tiled=True)
        out_all = out_all.reshape(chips, 2, width, features)
        out_same = lax.dynamic_index_in_dim(out_all, core, 1, False)
        out_other = lax.dynamic_index_in_dim(out_all, 1 - core, 1, False)
    out_same, out_other = out_same.reshape(shape), out_other.reshape(shape)
    out_mine = lax.dynamic_index_in_dim(out_same, my_wide // 2, 1, False).reshape(width, features)
    gate.second()
    up.second()
    attended_all, out_same, upstream, down_first = up.before(
        *gate.before(attended_all, out_same, out_grad[0], w_down)
    )
    grads_all = wide_gather(upstream)
    down = RowsGather(down_first, 1)
    tokens_all, after_all = out_project(
        core[None].astype(jnp.int32), attended_all, out_same, out_other, x_all, norms[2:]
    )
    tokens_all = down.before(tokens_all)
    after_attn = lax.dynamic_slice_in_dim(after_all, my_wide * local_len, local_len, 0)
    gate_part, up_part, hidden = gate_up_forward(tokens_all, gate, up)
    down.second()

    gate_grads, e_two = feed_back(grads_all, gate_part, up_part, down, gate, up)
    grad_normed_two = wide_scatter(e_two)
    gate_grads, hidden, tokens_all, grads_all = tie(gate_grads, hidden, tokens_all, grads_all)
    gate_grad = jnp.einsum("gtf,td->gfd", gate_grads, tokens_all, preferred_element_type=F).astype(B)
    down_grad = jnp.einsum("tf,td->fd", hidden, grads_all, preferred_element_type=F).astype(B)
    grad_down = RowsSum(down_grad, 1)
    grad_gate = RowsSum(gate_grad, 2)
    grad_normed_two = grad_gate.before(grad_down.before(grad_normed_two))
    hidden, *_ = tie(hidden, *grad_down.second(), *grad_gate.second())
    mlp_sum = LineSum(down_forward(hidden, down, features))
    mlp_sum.prepare()

    grad_after, branch, sums_two = norm_back(
        grad_normed_two, after_attn, out_grad[0], norms[2:3], True
    )
    branch_all = wide_gather(branch)
    branch_all = mlp_sum.before(branch_all)
    mlp_sum.advance()
    grad_attended = dotg(branch_all, out_mine, NT).astype(B)
    grad_proj, bias_grad = attend_back(
        q, k, v, grad_attended, lse, seg_col, seg_line, tables, heads
    )
    grad_proj = grad_gate.after(grad_down.after(grad_proj))
    grad_proj = mlp_sum.before(grad_proj)
    mlp_sum.prepare()
    mlp_sum.advance()
    e_one = dotg(grad_proj, w_mine, NT).astype(B)
    e_one, grad_proj = tie(e_one, grad_proj)
    grad_normed_one = wide_scatter(e_one)
    packed = weights_back(
        hat_all, grad_proj, w_mine, norms, sums_two, bias_grad, depth, norm_size
    )
    qkv_sum = RowsSum(packed, 0)
    branch_all = qkv_sum.before(branch_all)
    sent = qkv_sum.second()
    branch_all, *_ = tie(branch_all, *sent)
    grad_out = RowsSum(dotg(attended, branch_all, TN).astype(B), 0)
    qkv_sum.after(*grad_out.arrived_or_whole())
    grad_out.second()
    mlp_sum.before(qkv_sum.whole)
    mlp_sum.prepare()
    mlp_sum.advance()

    def late(first):
        outs = []
        for total in (grad_out, grad_gate, grad_down):
            first = total.after(*first)
            outs.append(total.result())
        if not strided:
            outs[0] = lax.ppermute(outs[0].astype(B), ("rows", "wide"), back).astype(F)
        grads = (outs[0], outs[1].swapaxes(1, 2), outs[2])
        steps = [
            adam_step(*parts)
            for parts in zip((w_out, gate_up, w_down), grads, (moment_out, moment_gate, moment_down))
        ]
        return grads + tuple(steps)

    received, late_values = wide_exchange(qkv_sum.result().astype(B), late)
    grad_out, grad_gate, grad_down, step_out, step_gate, step_down = late_values
    input_grad = norm_back(grad_normed_one, x_own, grad_after, norms[0:1], False)[0]

    received = mlp_sum.before(received)
    block_out = (after_attn + mlp_sum.result()).astype(B)
    received, input_grad = tie(received, input_grad)
    grad_qkv, step_qkv = finish(received, w_qkv, moment_qkv, strided)
    extra = received[:, depth : depth + 5].astype(F)
    grad_norms = jnp.sum(extra[:, :4, :norm_size], axis=0)
    bias_all = extra[:, 4].reshape(wide, 3, heads, HEAD_DIM)
    bias_all = bias_all.transpose((1, 2, 0, 3) if strided else (1, 0, 2, 3)).reshape(-1)
    grad_bias = lax.dynamic_slice_in_dim(
        bias_all, (my_row * wide + my_wide) * bias_size, bias_size, 0
    )

    return (
        block_out[None],
        input_grad[None],
        grad_norms,
        grad_qkv,
        grad_bias,
        grad_out,
        grad_gate,
        grad_down,
        adam_step(norm_params, grad_norms, moment_norm),
        step_qkv,
        adam_step(b_qkv, grad_bias, moment_bias),
        step_out,
        step_gate,
        step_down,
    )


def solution(mesh):
    both = ("rows", "wide")
    tokens = P("rows", "wide", None)
    weights = (P(None, both), P(both, None), P(both), P(both, None), P(None, "rows", "wide"), P("wide", "rows"))
    moments = tuple(P(None, *spec) for spec in weights)
    return jax.shard_map(
        shards,
        mesh=mesh,
        in_specs=(tokens, tokens, P("rows", None), P("rows", "wide")) + weights + moments,
        out_specs=(tokens, tokens) + weights + weights,
        check_vma=False,
    )
```

```python
import functools
import math

import jax
import jax.numpy as jnp
from jax import lax
from jax.experimental import pallas as pl
from jax.experimental.pallas import tpu as pltpu
from jax.sharding import PartitionSpec as P

F = jnp.float32
B = jnp.bfloat16
HEADS = 32
HEAD_DIM = 64
ROT_DIMS = 16
HALF_ROT = ROT_DIMS // 2
NORM_EPS = 1e-05
NEG_LARGE = -1e30
SCORE_SCALE = 0.125
ROPE_BASE = 10000.0
BETA_ONE = 0.9
BETA_TWO = 0.95
BIAS_FIRST = 0.999973438601112
BIAS_SECOND = 0.994079470779667
ADAM_EPS = 1e-08
DECAY_RATE = 0.1
TOKEN_BLOCK = 256
EXTRA_ROWS = 8
NT = (((1,), (1,)), ((), ()))
TN = (((0,), (0,)), ((), ()))


def dotg(left, right, dims):
    return lax.dot_general(left, right, dims, preferred_element_type=F)


def plus(left, right):
    return (left.astype(F) + right.astype(F)).astype(B)


def rows_swap(value, bits):
    return lax.ppermute(value, "rows", [(i, i ^ bits) for i in range(4)])


class RowsGather:
    def __init__(self, shard, axis):
        self.axis = axis
        self.size = shard.shape[axis]
        self.step = self.whole = None
        if lax.axis_size("rows") == 4:
            self.shard = shard
            self.step = (rows_swap(shard, 1), rows_swap(shard, 2))
        else:
            self.whole = lax.all_gather(shard, "rows", axis=axis, tiled=True)

    def before(self, *values):
        if self.step is not None:
            near, far, *values = tie(*self.step, *values)
            self.step = (near, far)
        return values if len(values) > 1 else values[0]

    def after(self, *values):
        if self.step is not None:
            self.step = tie(*self.step, *values)[:2]

    def second(self):
        if self.step is not None:
            self.near, self.far = self.step
            half = self.size // 2
            first = lax.slice_in_dim(self.near, 0, half, axis=self.axis)
            last = lax.slice_in_dim(self.far, half, self.size, axis=self.axis)
            self.step = (rows_swap(first, 2), rows_swap(last, 1))
        return self

    def pieces(self):
        if self.whole is not None:
            return [self.whole], [jnp.int32(0)]
        me = lax.axis_index("rows")
        places = [(me ^ bits) * self.size for bits in range(4)]
        arrays = [self.shard, self.near, self.far, *self.step]
        return arrays, places + [places[3] + self.size // 2]

    def join(self):
        if self.whole is not None:
            return self.whole
        shape = list(self.shard.shape)
        shape[self.axis] = 4 * self.size
        whole = jnp.zeros(shape, self.shard.dtype)
        for piece, place in zip(*self.pieces()):
            whole = lax.dynamic_update_slice_in_dim(whole, piece, place, self.axis)
        return whole


class RowsSum:
    def __init__(self, whole, axis):
        self.whole, self.axis = whole, axis
        self.arrived = self.sent = None
        if lax.axis_size("rows") == 4:
            diagonal = self.part(3)
            half = diagonal.shape[0] // 2
            self.arrived = (rows_swap(diagonal[:half], 1), rows_swap(diagonal[half:], 2))

    def part(self, bits):
        size = self.whole.shape[self.axis] // 4
        start = (lax.axis_index("rows") ^ bits) * size
        return lax.dynamic_slice_in_dim(self.whole, start, size, self.axis)

    def before(self, value):
        if self.arrived is not None:
            near, far, value = tie(*self.arrived, value)
            self.arrived = (near, far)
        return value

    def result(self):
        if self.arrived is None:
            return lax.psum_scatter(
                self.whole, "rows", scatter_dimension=self.axis, tiled=True
            ).astype(F)
        if self.sent is None:
            self.second()
        far, near = self.sent
        return self.part(0).astype(F) + far.astype(F) + near.astype(F)

    def arrived_or_whole(self):
        return (self.whole,) if self.arrived is None else self.arrived

    def second(self):
        if self.arrived is None:
            return self.whole, self.whole
        near, far = self.part(1), self.part(2)
        half = near.shape[0] // 2
        far = jnp.concatenate([plus(far[:half], self.arrived[0]), far[half:]], 0)
        near = jnp.concatenate([near[:half], plus(near[half:], self.arrived[1])], 0)
        self.sent = (rows_swap(far, 2), rows_swap(near, 1))
        return far, near

    def after(self, *values):
        if self.arrived is None:
            self.whole, *values = tie(self.whole, *values)
        else:
            far, near, *values = tie(*self.sent, *values)
            self.sent = (far, near)
        return values if len(values) > 1 else values[0]


def no_change(value):
    return jnp.minimum(jnp.abs(value[(0,) * value.ndim].astype(F)), 0.0)


class WideExchange:
    def __init__(self, blocks):
        self.shape = blocks.shape
        self.count = lax.axis_size("wide")
        me = lax.axis_index("wide")
        self.moved = []
        for step in range(self.count):
            block = lax.dynamic_slice_in_dim(blocks, (me + step) % self.count, 1, 0)
            if step:
                pairs = [(i, (i + step) % self.count) for i in range(self.count)]
                block = lax.ppermute(block, "wide", pairs)
            self.moved.append(block)

    def before(self, *values):
        half = self.count // 2
        self.moved[:half], values = split_tie(self.moved[:half], values)
        return values

    def join(self):
        me = lax.axis_index("wide")
        whole = jnp.zeros(self.shape, self.moved[0].dtype)
        for step, block in enumerate(self.moved):
            place = (me - step) % self.count
            whole = lax.dynamic_update_slice_in_dim(whole, block, place, 0)
        return whole


def wide_gather(shard):
    return lax.all_gather(shard, "wide", axis=0, tiled=True)


def wide_scatter(whole):
    return lax.psum_scatter(whole, "wide", scatter_dimension=0, tiled=True)


def tie(*values):
    return lax.optimization_barrier(values)


def split_tie(first, second):
    values = list(tie(*first, *second))
    return values[: len(first)], values[len(first) :]


def chip_pairs(move):
    pairs = []
    for at in range(lax.axis_size("wide")):
        target = move(at // 2, at % 2)
        if target is not None:
            pairs.append((at, target[0] * 2 + target[1]))
    return pairs


def core_swap(value):
    return lax.ppermute(value, "wide", chip_pairs(lambda chip, core: (chip, 1 - core)))


def rotated(value, same, ahead, behind):
    width = value.shape[1]
    return (
        value * same
        + pltpu.roll(value, width - HALF_ROT, 1) * ahead
        + pltpu.roll(value, HALF_ROT, 1) * behind
    )


def unrotated(value, same, ahead, behind):
    width = value.shape[1]
    return value * same - (
        pltpu.roll(value, width - HALF_ROT, 1) * ahead
        + pltpu.roll(value, HALF_ROT, 1) * behind
    )


def wide_tables(width, *refs):
    return [jnp.concatenate([ref[...]] * (width // ref.shape[1]), 1) for ref in refs]


def tables_body(col_ref, row_ref, same_ref, ahead_ref, behind_ref):
    tokens, lanes = same_ref.shape
    col = col_ref[...]
    before = jnp.zeros((tokens, 1), jnp.int32)
    for first in range(0, tokens, TOKEN_BLOCK):
        smaller = row_ref[:, first : first + TOKEN_BLOCK] < col
        before += jnp.sum(jnp.where(smaller, 1, 0), axis=1, keepdims=True)
    positions = lax.broadcasted_iota(jnp.int32, (tokens, 1), 0) - before
    dim = lax.broadcasted_iota(jnp.int32, (1, lanes), 1) % HEAD_DIM
    frequency = jnp.exp((dim % HALF_ROT).astype(F) * (-2.0 * math.log(ROPE_BASE) / ROT_DIMS))
    angles = positions.astype(F) * frequency
    cosine, sine = jnp.cos(angles), jnp.sin(angles)
    same_ref[...] = jnp.where(dim < ROT_DIMS, cosine, 1.0)
    ahead_ref[...] = jnp.where(dim < HALF_ROT, -sine, 0.0)
    behind_ref[...] = jnp.where((dim >= HALF_ROT) & (dim < ROT_DIMS), sine, 0.0)


def rotary_tables(seg_col, seg_line):
    tokens = seg_col.shape[0]
    return pl.pallas_call(
        tables_body,
        out_shape=[jax.ShapeDtypeStruct((tokens, 2 * HEAD_DIM), F)] * 3,
        name="tables",
    )(seg_col, seg_line)


def unit_rows(tensor):
    center = tensor - jnp.mean(tensor, axis=-1, keepdims=True)
    inverse = lax.rsqrt(jnp.mean(center * center, axis=-1, keepdims=True) + NORM_EPS)
    return center * inverse, inverse


def cost(products, values):
    return pl.CostEstimate(flops=2 * products, transcendentals=0, bytes_accessed=values)


def project_body(pieces, depth, norm_size, *refs):
    place_ref, x_ref, same_ref, ahead_ref, behind_ref = refs[:5]
    w_refs = refs[5 : 5 + pieces]
    q_ref, k_ref, v_ref, hat_ref, w_ref, norms_ref, bias_ref = refs[5 + pieces :]

    @pl.when(pl.program_id(0) == 0)
    def _():
        bias_ref[...] = jnp.zeros_like(bias_ref)
        for at, piece in enumerate(w_refs):
            blocks = piece.shape[0]
            rows = pl.multiple_of(place_ref[at] * depth, blocks * depth)
            columns = pl.multiple_of(place_ref[at] * norm_size, blocks * norm_size)
            for block in range(blocks):
                w_ref[pl.ds(rows + block * depth, depth), :] = piece[block, :depth]
                bias_ref[...] += piece[block, depth + 4 : depth + 5].astype(F)
            norms = [piece[block, depth : depth + 4, :norm_size].astype(F) for block in range(blocks)]
            norms_ref[:, pl.ds(columns, blocks * norm_size)] = jnp.concatenate(norms, 1)

    hat, _ = unit_rows(x_ref[...].astype(F))
    normed = (hat * norms_ref[0:1, :] + norms_ref[1:2, :]).astype(B)
    hat_ref[...] = hat.astype(B)
    out = jnp.dot(normed, w_ref[...], preferred_element_type=F) + bias_ref[...]
    width = q_ref.shape[1]
    tables = wide_tables(width, same_ref, ahead_ref, behind_ref)
    q_ref[...] = rotated(out[:, :width], *tables).astype(B)
    k_ref[...] = rotated(out[:, width : 2 * width], *tables).astype(B)
    v_ref[...] = out[:, 2 * width :].astype(B)


def row_spec(width, block):
    return pl.BlockSpec((block, width), lambda i: (i, 0))


def whole_spec(array):
    return pl.BlockSpec(array.shape, lambda i: (0, 0))


def project(x_all, gathered, tables, depth, norm_size):
    tokens, features = x_all.shape
    pieces, places = gathered.pieces()
    columns = pieces[0].shape[2]
    width = columns // 3
    block = min(TOKEN_BLOCK, tokens)
    row = lambda size: pl.BlockSpec((block, size), lambda i, place: (i, 0))
    flat = lambda *shape: pl.BlockSpec(shape, lambda i, place: (0,) * len(shape))
    return pl.pallas_call(
        functools.partial(project_body, len(pieces), depth, norm_size),
        grid_spec=pltpu.PrefetchScalarGridSpec(
            num_scalar_prefetch=1,
            grid=(tokens // block,),
            in_specs=[row(features)]
            + [row(table.shape[1]) for table in tables]
            + [flat(*piece.shape) for piece in pieces],
            out_specs=[row(width)] * 3
            + [row(features), flat(features, columns), flat(4, features), flat(1, columns)],
        ),
        out_shape=[jax.ShapeDtypeStruct((tokens, width), B)] * 3
        + [
            jax.ShapeDtypeStruct((tokens, features), B),
            jax.ShapeDtypeStruct((features, columns), B),
            jax.ShapeDtypeStruct((4, features), F),
            jax.ShapeDtypeStruct((1, columns), F),
        ],
        name="project",
        cost_estimate=cost(tokens * features * columns, 4 * tokens * features),
    )(jnp.stack(places), x_all, *tables, *pieces)


def gate_body(pieces, *refs):
    place_ref, tokens_ref = refs[:2]
    gate_ref, up_ref, hidden_ref = refs[2 + 2 * pieces :]
    sums = []
    for half in range(2):
        total = jnp.zeros(gate_ref.shape, F)
        for at in range(pieces):
            w_ref = refs[2 + half * pieces + at]
            size = w_ref.shape[1]
            columns = pl.ds(pl.multiple_of(place_ref[at], size), size)
            total += dotg(tokens_ref[:, columns], w_ref[...], NT)
        sums.append(total)
    gate_ref[...] = sums[0]
    up_ref[...] = sums[1]
    hidden_ref[...] = (sums[0] * jax.nn.sigmoid(sums[0]) * sums[1]).astype(B)


def piece_call(body, name, places, blocked, pieces, outs, products):
    tokens = blocked[0].shape[0]
    block = min(TOKEN_BLOCK, tokens)

    def spec(shape):
        if len(shape) == 3:
            return pl.BlockSpec((shape[0], block, shape[2]), lambda i, place: (0, i, 0))
        return pl.BlockSpec((block, shape[1]), lambda i, place: (i, 0))

    size = sum(array.size * array.dtype.itemsize for array in blocked + pieces)
    return pl.pallas_call(
        functools.partial(body, len(places)),
        grid_spec=pltpu.PrefetchScalarGridSpec(
            num_scalar_prefetch=1,
            grid=(tokens // block,),
            in_specs=[spec(array.shape) for array in blocked]
            + [pl.BlockSpec(piece.shape, lambda i, place: (0, 0)) for piece in pieces],
            out_specs=[spec(out.shape) for out in outs],
        ),
        out_shape=outs,
        name=name,
        cost_estimate=cost(products, size),
    )(jnp.stack(places), *blocked, *pieces)


def gate_up_forward(tokens_all, gate, up):
    tokens = tokens_all.shape[0]
    gates, places = gate.pieces()
    ups, _ = up.pieces()
    units = gates[0].shape[0]
    outs = [jax.ShapeDtypeStruct((tokens, units), kind) for kind in (F, F, B)]
    products = 2 * tokens * units * tokens_all.shape[1]
    return piece_call(gate_body, "gate_up", places, [tokens_all], gates + ups, outs, products)


def down_body(pieces, *refs):
    place_ref, hidden_ref = refs[:2]
    out_ref = refs[2 + pieces]
    for at in range(pieces):
        w_ref = refs[2 + at]
        size = w_ref.shape[1]
        columns = pl.ds(pl.multiple_of(place_ref[at], size), size)
        out_ref[:, columns] = jnp.dot(
            hidden_ref[...], w_ref[...], preferred_element_type=F
        ).astype(B)


def down_forward(hidden, down, features):
    tokens, units = hidden.shape
    downs, places = down.pieces()
    outs = [jax.ShapeDtypeStruct((tokens, features), B)]
    return piece_call(
        down_body, "down", places, [hidden], downs, outs, tokens * units * features
    )[0]


def feed_back_body(pieces, *refs):
    place_ref, grads_ref, gate_ref, up_ref = refs[:4]
    weights = refs[4 : 4 + 3 * pieces]
    out_ref, e_ref = refs[4 + 3 * pieces :]
    grad_hidden = jnp.zeros(gate_ref.shape, F)
    for at in range(pieces):
        size = weights[at].shape[1]
        columns = pl.ds(pl.multiple_of(place_ref[at], size), size)
        grad_hidden += dotg(grads_ref[:, columns], weights[at][...], NT)
    gate = gate_ref[...]
    sigmoid = jax.nn.sigmoid(gate)
    grad_gate = grad_hidden * up_ref[...] * sigmoid * (1.0 + gate * (1.0 - sigmoid))
    grad_gate = grad_gate.astype(B)
    grad_up = (grad_hidden * (gate * sigmoid)).astype(B)
    out_ref[0] = grad_gate
    out_ref[1] = grad_up
    for at in range(pieces):
        size = weights[at].shape[1]
        columns = pl.ds(pl.multiple_of(place_ref[at], size), size)
        e = jnp.dot(grad_gate, weights[pieces + at][...], preferred_element_type=F)
        e += jnp.dot(grad_up, weights[2 * pieces + at][...], preferred_element_type=F)
        e_ref[:, columns] = e.astype(B)


def feed_back(grads_all, gate_part, up_part, down, gate, up):
    tokens, features = grads_all.shape
    units = gate_part.shape[1]
    downs, places = down.pieces()
    outs = [
        jax.ShapeDtypeStruct((2, tokens, units), B),
        jax.ShapeDtypeStruct((tokens, features), B),
    ]
    weights = downs + gate.pieces()[0] + up.pieces()[0]
    return piece_call(
        feed_back_body,
        "feed_back",
        places,
        [grads_all, gate_part, up_part],
        weights,
        outs,
        3 * tokens * units * features,
    )


def pair_bias(seg_col, seg_row, first, size, keys):
    same = seg_col[first : first + size, :] == seg_row[:, :keys]
    key_pos = lax.broadcasted_iota(jnp.int32, (size, keys), 1)
    query_pos = first + lax.broadcasted_iota(jnp.int32, (size, keys), 0)
    return jnp.where(same & (key_pos <= query_pos), 0.0, NEG_LARGE)


def head_masks(heads, width):
    lane = lax.broadcasted_iota(jnp.int32, (1, width), 1) // HEAD_DIM
    return [jnp.where(lane == head, 1.0, 0.0).astype(B) for head in range(heads)]


def attend_body(heads, q_ref, k_ref, v_ref, seg_col, seg_row, out_ref, lse_ref):
    tokens, width = q_ref.shape
    block = min(TOKEN_BLOCK, tokens)
    masks = head_masks(heads, width)
    for first in range(0, tokens, block):
        keys = first + block
        bias = pair_bias(seg_col, seg_row, first, block, keys)
        queries = q_ref[first:keys, :]
        total = jnp.zeros((block, width), F)
        for head in range(heads):
            scores = dotg(queries * (masks[head] * SCORE_SCALE), k_ref[:keys, :], NT) + bias
            top = jnp.max(scores, axis=-1, keepdims=True)
            weights = jnp.exp(scores - top)
            norm = jnp.sum(weights, axis=-1, keepdims=True)
            probs = (weights * (1.0 / norm)).astype(B)
            total += jnp.dot(probs, v_ref[:keys, :] * masks[head], preferred_element_type=F)
            lse_ref[first:keys, head : head + 1] = top + jnp.log(norm)
        out_ref[first:keys, :] = total.astype(B)


def attend(q, k, v, seg_col, seg_row, heads):
    tokens, width = q.shape
    return pl.pallas_call(
        functools.partial(attend_body, heads),
        out_shape=[
            jax.ShapeDtypeStruct((tokens, width), B),
            jax.ShapeDtypeStruct((tokens, 128), F),
        ],
        name="attend",
        cost_estimate=cost(heads * tokens * tokens * 512, 8 * tokens * width),
    )(q, k, v, seg_col, seg_row)


def out_project_body(pieces, *refs):
    at_ref, place_ref, attended_ref, x_ref, norm_ref = refs[:5]
    piece_refs = (refs[5 : 5 + pieces], refs[5 + pieces : 5 + 2 * pieces])
    normed_ref, after_ref, mine_ref, w_ref = refs[5 + 2 * pieces :]
    core = at_ref[0]
    _, chips, width, features = w_ref.shape

    @pl.when(pl.program_id(0) == 0)
    def _():
        for same, group in enumerate(piece_refs):
            for at, piece in enumerate(group):
                place = place_ref[at]
                whole = group[0].shape[0]
                size = width * whole // (chips * width) if pieces == 1 else whole // chips
                held = piece.shape[0] // size
                slot = place // whole
                first = place % whole // size
                for chip in range(held):
                    rows = pl.ds(pl.multiple_of(slot * size, size), size)
                    w_ref[same, first + chip, rows, :] = piece[chip * size : (chip + 1) * size]
        mine_ref[...] = w_ref[0, at_ref[1]]

    total = x_ref[...].astype(F)
    for chip in range(chips):
        for same, which in enumerate((core, 1 - core)):
            total += jnp.dot(
                attended_ref[chip * 2 + which], w_ref[same, chip], preferred_element_type=F
            )
    after_ref[...] = total
    hat, _ = unit_rows(total)
    normed_ref[...] = (hat * norm_ref[0:1, :] + norm_ref[1:2, :]).astype(B)


def out_project(at, attended_all, same, other, places, x_all, norm_two):
    owners, tokens, width = attended_all.shape
    features = x_all.shape[1]
    block = min(TOKEN_BLOCK, tokens)
    flat = lambda array: pl.BlockSpec(array.shape, lambda i, at, place: (0, 0))
    rows = pl.BlockSpec((block, features), lambda i, at, place: (i, 0))
    return pl.pallas_call(
        functools.partial(out_project_body, len(same)),
        grid_spec=pltpu.PrefetchScalarGridSpec(
            num_scalar_prefetch=2,
            grid=(tokens // block,),
            in_specs=[
                pl.BlockSpec((owners, block, width), lambda i, at, place: (0, i, 0)),
                rows,
                flat(norm_two),
            ]
            + [flat(piece) for piece in same + other],
            out_specs=[
                rows,
                rows,
                pl.BlockSpec((width, features), lambda i, at, place: (0, 0)),
            ],
            scratch_shapes=[pltpu.VMEM((2, owners // 2, width, features), B)],
        ),
        out_shape=[
            jax.ShapeDtypeStruct((tokens, features), B),
            jax.ShapeDtypeStruct((tokens, features), F),
            jax.ShapeDtypeStruct((width, features), B),
        ],
        name="out_project",
        cost_estimate=cost(tokens * features * features, 8 * tokens * features),
    )(
        jnp.stack(at).astype(jnp.int32),
        jnp.stack(places).astype(jnp.int32),
        attended_all,
        x_all,
        norm_two,
        *same,
        *other,
    )


def attend_back_body(
    heads, q_ref, k_ref, v_ref, g_ref, lse_ref, seg_col, seg_row, same_ref, ahead_ref, behind_ref,
    out_ref, bias_ref, dq_ref, dk_ref, dv_ref,
):
    tokens, width = q_ref.shape
    block = min(TOKEN_BLOCK, tokens)
    masks = head_masks(heads, width)
    for first in reversed(range(0, tokens, block)):
        keys = first + block
        bias = pair_bias(seg_col, seg_row, first, block, keys)
        queries = q_ref[first:keys, :]
        grads = g_ref[first:keys, :]
        dq = jnp.zeros((block, width), F)
        stacks = ([], [], [], [])
        for head in range(heads):
            q_head = queries * (masks[head] * SCORE_SCALE)
            g_head = grads * masks[head]
            scores = dotg(q_head, k_ref[:keys, :], NT) + bias
            probs = jnp.exp(scores - lse_ref[first:keys, head : head + 1])
            weighted = probs * dotg(g_head, v_ref[:keys, :], NT)
            delta = jnp.sum(weighted, axis=-1, keepdims=True)
            grad_scores = (weighted - probs * delta).astype(B)
            dq += jnp.dot(grad_scores, k_ref[:keys, :] * masks[head], preferred_element_type=F)
            for stack, value in zip(stacks, (grad_scores, q_head, probs.astype(B), g_head)):
                stack.append(value)
        joined = [jnp.concatenate(stack, 0) for stack in stacks]
        dk = dotg(joined[0], joined[1], TN)
        dv = dotg(joined[2], joined[3], TN)
        if keys == tokens:
            dk_ref[...] = dk
            dv_ref[...] = dv
        else:
            dk_ref[:keys, :] += dk
            dv_ref[:keys, :] += dv
        dq_ref[first:keys, :] = dq * SCORE_SCALE
    tables = wide_tables(width, same_ref, ahead_ref, behind_ref)
    pieces = (unrotated(dq_ref[...], *tables), unrotated(dk_ref[...], *tables), dv_ref[...])
    for at, piece in enumerate(pieces):
        rounded = piece.astype(B)
        out_ref[:, at * width : (at + 1) * width] = rounded
        bias_ref[:, at * width : (at + 1) * width] = jnp.sum(
            rounded.astype(F), axis=0, keepdims=True
        )


def attend_back(q, k, v, grads, lse, seg_col, seg_row, tables, heads):
    tokens, width = q.shape
    return pl.pallas_call(
        functools.partial(attend_back_body, heads),
        out_shape=[
            jax.ShapeDtypeStruct((tokens, 3 * width), B),
            jax.ShapeDtypeStruct((1, 3 * width), F),
        ],
        scratch_shapes=[pltpu.VMEM((tokens, width), F)] * 3,
        name="attend_back",
        cost_estimate=cost(heads * tokens * tokens * 1024, 16 * tokens * width),
    )(q, k, v, grads, lse, seg_col, seg_row, *tables)


def weights_back_body(
    depth, norm_size, hat_ref, grad_ref, w_ref, norms_ref, two_ref, bias_ref, out_ref
):
    blocks, rows, columns = out_ref.shape
    product = dotg(hat_ref[...], grad_ref[...], TN)
    weights = w_ref[...].astype(F)
    bias = bias_ref[...]
    gain = jnp.sum(product * weights, axis=1, keepdims=True)
    shift = jnp.sum(weights * bias, axis=1, keepdims=True)
    lanes = lax.broadcasted_iota(jnp.int32, (gain.shape[0], 128), 1)
    ones = jnp.where(lanes == 0, gain, shift).T
    norms = jnp.concatenate([norms_ref[...]] * 2, 0).T
    product = (product * norms[:, 0:1] + norms[:, 1:2] * bias).astype(B)
    sums = jnp.concatenate([ones[:2], two_ref[...]], 0).astype(B)
    bias = bias.astype(B)
    for block in range(blocks):
        out_ref[block, :depth, :] = product[block * depth : (block + 1) * depth]
        mine = sums[:, block * norm_size : (block + 1) * norm_size]
        out_ref[block, depth:, :] = jnp.concatenate(
            [
                jnp.concatenate([mine, jnp.zeros((4, columns - norm_size), B)], 1),
                bias,
                jnp.zeros((rows - depth - 5, columns), B),
            ],
            0,
        )


def weights_back(hat_all, grad_proj, w_mine, norms, two, bias_grad, depth, norm_size):
    tokens, features = hat_all.shape
    columns = grad_proj.shape[1]
    block = min(512, features)
    flat = lambda array: pl.BlockSpec(array.shape, lambda i: (0, 0))
    across = lambda rows: pl.BlockSpec((rows, block), lambda i: (0, i))
    return pl.pallas_call(
        functools.partial(weights_back_body, depth, norm_size),
        grid=(features // block,),
        in_specs=[
            across(tokens),
            flat(grad_proj),
            row_spec(columns, block),
            across(4),
            across(2),
            flat(bias_grad),
        ],
        out_specs=pl.BlockSpec((block // depth, depth + EXTRA_ROWS, columns), lambda i: (i, 0, 0)),
        out_shape=jax.ShapeDtypeStruct((features // depth, depth + EXTRA_ROWS, columns), B),
        name="weights_back",
        cost_estimate=cost(tokens * features * columns, 4 * tokens * features),
    )(hat_all, grad_proj, w_mine, norms, two, bias_grad)


def norm_back_body(e_ref, x_ref, upstream_ref, gain_ref, grad_ref, *refs):
    hat, inverse = unit_rows(x_ref[...].astype(F))
    e = e_ref[...].astype(F)
    scaled = e * gain_ref[...]
    mean_grad = jnp.mean(scaled, axis=-1, keepdims=True)
    mean_proj = jnp.mean(scaled * hat, axis=-1, keepdims=True)
    grad = upstream_ref[...].astype(F) + inverse * (scaled - mean_grad - hat * mean_proj)
    grad_ref[...] = grad
    if refs:
        rounded_ref, sums_ref = refs
        rounded_ref[...] = grad.astype(B)
        sums_ref[...] = jnp.concatenate(
            [jnp.sum(e * hat, axis=0, keepdims=True), jnp.sum(e, axis=0, keepdims=True)], 0
        )


def norm_back(e, x, upstream, gain, more):
    tokens, features = x.shape
    outs = [jax.ShapeDtypeStruct((tokens, features), F)]
    if more:
        outs += [jax.ShapeDtypeStruct((tokens, features), B), jax.ShapeDtypeStruct((2, features), F)]
    return pl.pallas_call(norm_back_body, out_shape=outs, name="norm_back")(e, x, upstream, gain)


def pack_body(strided, me_ref, w_ref, norm_ref, bias_ref, out_ref):
    wide, _, columns = out_ref.shape
    depth = w_ref.shape[0]
    third = w_ref.shape[1] // 3
    width = columns // 3
    me = me_ref[0]
    held = bias_ref.shape[1]
    padded = jnp.concatenate(
        [norm_ref[...], jnp.zeros((4, columns - norm_ref.shape[1]), B)], 1
    )
    for owner in range(wide):
        biases = []
        for part in range(3):
            for slot in range(width // HEAD_DIM):
                head = slot * wide + owner if strided else owner * (width // HEAD_DIM) + slot
                first = part * third + head * HEAD_DIM
                if slot % 2 == 0:
                    left = w_ref[:, first : first + HEAD_DIM]
                else:
                    to = part * width + (slot - 1) * HEAD_DIM
                    out_ref[owner, :depth, to : to + 2 * HEAD_DIM] = jnp.concatenate(
                        [left, w_ref[:, first : first + HEAD_DIM]], 1
                    )
                last = first + HEAD_DIM
                while first < last:
                    stop = min(last, (first // held + 1) * held)
                    mine = bias_ref[:, first % held : first % held + stop - first]
                    kept = jnp.where(me == first // held, mine.astype(F), 0.0)
                    biases.append(kept.astype(B))
                    first = stop
        out_ref[owner, depth:, :] = jnp.concatenate(
            [padded, jnp.concatenate(biases, 1), jnp.zeros((EXTRA_ROWS - 5, columns), B)], 0
        )


def pack(me, w_qkv, norm_params, b_qkv, strided, wide):
    depth, columns = w_qkv.shape
    memory = [pltpu.SMEM] + [pltpu.VMEM] * 3
    return pl.pallas_call(
        functools.partial(pack_body, strided),
        in_specs=[pl.BlockSpec(memory_space=space) for space in memory],
        out_shape=jax.ShapeDtypeStruct((wide, depth + EXTRA_ROWS, columns // wide), B),
        name="pack",
    )(me[None].astype(jnp.int32), w_qkv, norm_params, b_qkv[None])


def adam_step(parameter, gradient, moments):
    first_moment = BETA_ONE * moments[0] + (1.0 - BETA_ONE) * gradient
    second_moment = BETA_TWO * moments[1] + (1.0 - BETA_TWO) * gradient * gradient
    return first_moment / BIAS_FIRST / (
        jnp.sqrt(second_moment / BIAS_SECOND) + ADAM_EPS
    ) + DECAY_RATE * parameter.astype(F)


def finish_body(strided, wide, got_ref, w_ref, moment_ref, grad_ref, step_ref):
    depth = w_ref.shape[0]
    third = w_ref.shape[1] // 3
    width = got_ref.shape[2] // 3
    for part in range(3):
        for at in range(third // 128):
            if strided:
                slot, owner = at * 2 // wide, at * 2 % wide
                first = part * width + slot * HEAD_DIM
                gradient = jnp.concatenate(
                    [got_ref[owner + k, :depth, first : first + HEAD_DIM] for k in range(2)], 1
                )
            else:
                owner, first = at * 128 // width, part * width + at * 128 % width
                gradient = got_ref[owner, :depth, first : first + 128]
            gradient = gradient.astype(F)
            columns = slice(part * third + at * 128, part * third + at * 128 + 128)
            grad_ref[:, columns] = gradient
            step_ref[:, columns] = adam_step(
                w_ref[:, columns], gradient, (moment_ref[0, :, columns], moment_ref[1, :, columns])
            )


def finish(received, w_qkv, moments, strided):
    return pl.pallas_call(
        functools.partial(finish_body, strided, received.shape[0]),
        out_shape=[jax.ShapeDtypeStruct(w_qkv.shape, F)] * 2,
        name="finish",
    )(received, w_qkv, moments)


def shards(
    block_input, out_grad, segment_ids, positions, norm_params, w_qkv, b_qkv, w_out, gate_up, w_down,
    moment_norm, moment_qkv, moment_bias, moment_out, moment_gate, moment_down,
):
    x_own = block_input[0]
    local_len, features = x_own.shape
    rows = lax.axis_size("rows")
    wide = lax.axis_size("wide")
    my_row = lax.axis_index("rows")
    my_wide = lax.axis_index("wide")
    segment_row = segment_ids[0]
    heads = HEADS // wide
    width = heads * HEAD_DIM
    depth = w_qkv.shape[0]
    norm_size = norm_params.shape[1]
    strided = depth == HEAD_DIM

    bias_size = b_qkv.shape[0]
    chips = wide // 2
    core = my_wide % 2
    blocks = range(rows * wide)
    back = [(b % rows * wide + b // rows, b) for b in blocks]
    gate_first = gate_up.swapaxes(1, 2)
    gate = RowsGather(gate_first[0], 1)
    exchange = WideExchange(
        pack(my_row * wide + my_wide, w_qkv, norm_params, b_qkv, strided, wide)
    )
    segment_row, *arrived = exchange.before(segment_row, *(gate.step or ()))
    gate.step = arrived or None
    received, x_first = tie(exchange.join(), x_own)
    x_all = wide_gather(x_first)
    w_rows = RowsGather(received, 0)
    seg_col = segment_row[:, None]
    seg_line = segment_row[None, :]
    tables = w_rows.before(*rotary_tables(seg_col, seg_line))
    w_rows.second()
    if gate.step:
        up_first, *gate.step = w_rows.before(gate_first[1], *gate.step)
    else:
        up_first = gate_first[1]
    up = RowsGather(up_first, 1)
    gate.second()
    if strided:
        x_all, out_first = w_rows.before(x_all, w_out)
        out_line = lax.all_gather(out_first, "wide", axis=0, tiled=False)
    q, k, v, hat_all, w_mine, norms, _ = project(x_all, w_rows, tables, depth, norm_size)
    attended, lse = attend(q, k, v, seg_col, seg_line, heads)
    attended = gate.before(up.before(attended))
    if strided:
        attended, out_line = tie(attended, out_line)
    attended_all = lax.all_gather(attended, "wide", axis=0, tiled=False)
    if strided:
        out_line = out_line.reshape(chips, 2, depth, features)
        out_line = lax.dynamic_index_in_dim(out_line, core, 1, False)
        out_rows = RowsGather(out_line.reshape(chips * depth, features), 0)
        out_rows.second()
        out_rows.step = up.before(*out_rows.step) if out_rows.step else None
        out_pieces, out_places = out_rows.pieces()
    else:
        out_all = lax.all_gather(w_out, ("rows", "wide"), axis=0, tiled=True)
        out_all = out_all.reshape(chips, 2, width, features)
        out_line = lax.dynamic_index_in_dim(out_all, core, 1, False)
        out_pieces, out_places = [out_line.reshape(chips * width, features)], [jnp.int32(0)]
    swapped = [core_swap(piece) for piece in out_pieces]
    up.second()
    attended_all, upstream, down_first, *swapped = tie(
        attended_all, out_grad[0], w_down, *swapped
    )
    down = RowsGather(down_first, 1)
    grads_all = wide_gather(upstream)
    tokens_all, after_all, out_mine = out_project(
        (core, my_wide // 2), attended_all, out_pieces, swapped, out_places, x_all, norms[2:]
    )
    tokens_all = down.before(tokens_all)
    down.second()
    after_attn = lax.dynamic_slice_in_dim(after_all, my_wide * local_len, local_len, 0)
    gate_part, up_part, hidden = gate_up_forward(tokens_all, gate, up)

    gate_grads, e_two = feed_back(grads_all, gate_part, up_part, down, gate, up)
    grad_normed_two = wide_scatter(e_two)
    gate_grads, hidden, tokens_all, grads_all = tie(gate_grads, hidden, tokens_all, grads_all)
    gate_grad = jnp.einsum("gtf,td->gfd", gate_grads, tokens_all, preferred_element_type=F).astype(B)
    down_grad = jnp.einsum("tf,td->fd", hidden, grads_all, preferred_element_type=F).astype(B)
    grad_down = RowsSum(down_grad, 1)
    grad_gate = RowsSum(gate_grad, 2)
    grad_normed_two = grad_gate.before(grad_down.before(grad_normed_two))
    hidden, *_ = tie(hidden, *grad_down.second(), *grad_gate.second())
    mlp_part = down_forward(hidden, down, features)

    grad_after, branch, sums_two = norm_back(
        grad_normed_two, after_attn, out_grad[0], norms[2:3], True
    )
    branch_all = wide_gather(branch)
    mlp_part, branch_all = grad_gate.after(mlp_part, branch_all)
    mlp_out = wide_scatter(mlp_part)
    grad_attended = dotg(branch_all, out_mine, NT).astype(B)
    grad_proj, bias_grad = attend_back(
        q, k, v, grad_attended, lse, seg_col, seg_line, tables, heads
    )
    grad_proj = grad_down.after(grad_proj)
    e_one = dotg(grad_proj, w_mine, NT).astype(B)
    e_one, grad_proj, branch_all = tie(e_one, grad_proj, branch_all)
    grad_normed_one = wide_scatter(e_one)
    grad_out = RowsSum(dotg(attended, branch_all, TN).astype(B), 0)
    packed = weights_back(
        hat_all, grad_proj, w_mine, norms, sums_two, bias_grad, depth, norm_size
    )
    qkv_sum = RowsSum(packed, 0)
    qkv_sum.whole = grad_out.before(qkv_sum.whole)
    grad_out.second()
    start = no_change(qkv_sum.second()[0])
    mlp_out = qkv_sum.after(mlp_out)
    exchange = WideExchange(qkv_sum.result().astype(B))
    grad_out = grad_out.result() + start
    if not strided:
        grad_out = lax.ppermute(grad_out.astype(B), ("rows", "wide"), back).astype(F)
    grad_down = grad_down.result() + start
    grad_gate = (grad_gate.result() + start).swapaxes(1, 2)
    step_out = adam_step(w_out, grad_out, moment_out)
    step_gate = adam_step(gate_up, grad_gate, moment_gate)
    step_down = adam_step(w_down, grad_down, moment_down)
    received = exchange.join()

    block_out = (after_attn + mlp_out.astype(F)).astype(B)
    grad_qkv, step_qkv = finish(received, w_qkv, moment_qkv, strided)
    grad_qkv, step_qkv, grad_normed_one = tie(grad_qkv, step_qkv, grad_normed_one)
    input_grad = norm_back(grad_normed_one, x_own, grad_after, norms[0:1], False)[0]
    extra = received[:, depth : depth + 5].astype(F)
    grad_norms = jnp.sum(extra[:, :4, :norm_size], axis=0)
    bias_all = extra[:, 4].reshape(wide, 3, heads, HEAD_DIM)
    bias_all = bias_all.transpose((1, 2, 0, 3) if strided else (1, 0, 2, 3)).reshape(-1)
    grad_bias = lax.dynamic_slice_in_dim(
        bias_all, (my_row * wide + my_wide) * bias_size, bias_size, 0
    )

    return (
        block_out[None],
        input_grad[None],
        grad_norms,
        grad_qkv,
        grad_bias,
        grad_out,
        grad_gate,
        grad_down,
        adam_step(norm_params, grad_norms, moment_norm),
        step_qkv,
        adam_step(b_qkv, grad_bias, moment_bias),
        step_out,
        step_gate,
        step_down,
    )


def solution(mesh):
    both = ("rows", "wide")
    tokens = P("rows", "wide", None)
    weights = (P(None, both), P(both, None), P(both), P(both, None), P(None, "rows", "wide"), P("wide", "rows"))
    moments = tuple(P(None, *spec) for spec in weights)
    return jax.shard_map(
        shards,
        mesh=mesh,
        in_specs=(tokens, tokens, P("rows", None), P("rows", "wide")) + weights + moments,
        out_specs=(tokens, tokens) + weights + weights,
        check_vma=False,
    )
```

```python
import functools
import math

import jax
import jax.numpy as jnp
from jax import lax
from jax.experimental import pallas as pl
from jax.experimental.pallas import tpu as pltpu
from jax.sharding import PartitionSpec as P

F = jnp.float32
B = jnp.bfloat16
HEADS = 32
HEAD_DIM = 64
ROT_DIMS = 16
HALF_ROT = ROT_DIMS // 2
NORM_EPS = 1e-05
NEG_LARGE = -1e30
SCORE_SCALE = 0.125
ROPE_BASE = 10000.0
BETA_ONE = 0.9
BETA_TWO = 0.95
BIAS_FIRST = 0.999973438601112
BIAS_SECOND = 0.994079470779667
ADAM_EPS = 1e-08
DECAY_RATE = 0.1
TOKEN_BLOCK = 256
FEED_BLOCK = 512
EXTRA_ROWS = 8
NT = (((1,), (1,)), ((), ()))
TN = (((0,), (0,)), ((), ()))


def dotg(left, right, dims):
    return lax.dot_general(left, right, dims, preferred_element_type=F)


def plus(left, right):
    return (left.astype(F) + right.astype(F)).astype(B)


def rows_swap(value, bits):
    return lax.ppermute(value, "rows", [(i, i ^ bits) for i in range(4)])


class RowsGather:
    def __init__(self, shard, axis):
        self.axis = axis
        self.size = shard.shape[axis]
        self.step = self.whole = self.sends = None
        if lax.axis_size("rows") == 4:
            self.shard = shard
            self.step = (rows_swap(shard, 1), rows_swap(shard, 2))
        else:
            self.whole = lax.all_gather(shard, "rows", axis=axis, tiled=True)

    def before(self, *values):
        if self.step is not None:
            near, far, *values = tie(*self.step, *values)
            self.step = (near, far)
        return values if len(values) > 1 else values[0]

    def after(self, *values):
        if self.step is not None:
            self.step = tie(*self.step, *values)[:2]

    def halves(self, *values):
        if self.step is not None:
            self.near, self.far = self.step
            half = self.size // 2
            first = lax.slice_in_dim(self.near, 0, half, axis=self.axis)
            last = lax.slice_in_dim(self.far, half, self.size, axis=self.axis)
            first, last, *values = tie(first, last, *values) if values else (first, last)
            self.sends = (first, last)
        return values if len(values) > 1 else values[0] if values else None

    def second(self):
        if self.step is not None:
            if self.sends is None:
                self.halves()
            self.step = (rows_swap(self.sends[0], 2), rows_swap(self.sends[1], 1))
        return self

    def pieces(self):
        if self.whole is not None:
            return [self.whole], [jnp.int32(0)]
        me = lax.axis_index("rows")
        places = [(me ^ bits) * self.size for bits in range(4)]
        arrays = [self.shard, self.near, self.far, *self.step]
        return arrays, places + [places[3] + self.size // 2]

    def join(self):
        if self.whole is not None:
            return self.whole
        shape = list(self.shard.shape)
        shape[self.axis] = 4 * self.size
        whole = jnp.zeros(shape, self.shard.dtype)
        for piece, place in zip(*self.pieces()):
            whole = lax.dynamic_update_slice_in_dim(whole, piece, place, self.axis)
        return whole


class RowsSum:
    def __init__(self, whole, axis):
        self.whole, self.axis = whole, axis
        self.arrived = self.sent = None
        if lax.axis_size("rows") == 4:
            diagonal = self.part(3)
            half = diagonal.shape[0] // 2
            self.arrived = (rows_swap(diagonal[:half], 1), rows_swap(diagonal[half:], 2))

    def part(self, bits):
        size = self.whole.shape[self.axis] // 4
        start = (lax.axis_index("rows") ^ bits) * size
        return lax.dynamic_slice_in_dim(self.whole, start, size, self.axis)

    def before(self, value):
        if self.arrived is not None:
            near, far, value = tie(*self.arrived, value)
            self.arrived = (near, far)
        return value

    def result(self):
        if self.arrived is None:
            return lax.psum_scatter(
                self.whole, "rows", scatter_dimension=self.axis, tiled=True
            ).astype(F)
        if self.sent is None:
            self.second()
        far, near = self.sent
        return self.part(0).astype(F) + far.astype(F) + near.astype(F)

    def arrived_or_whole(self):
        return (self.whole,) if self.arrived is None else self.arrived

    def second(self):
        if self.arrived is None:
            return self.whole, self.whole
        near, far = self.part(1), self.part(2)
        half = near.shape[0] // 2
        far = jnp.concatenate([plus(far[:half], self.arrived[0]), far[half:]], 0)
        near = jnp.concatenate([near[:half], plus(near[half:], self.arrived[1])], 0)
        self.sent = (rows_swap(far, 2), rows_swap(near, 1))
        return far, near

    def after(self, *values):
        if self.arrived is None:
            self.whole, *values = tie(self.whole, *values)
        else:
            far, near, *values = tie(*self.sent, *values)
            self.sent = (far, near)
        return values if len(values) > 1 else values[0]


def no_change(value):
    return jnp.minimum(jnp.abs(value[(0,) * value.ndim].astype(F)), 0.0)


class WideExchange:
    def __init__(self, blocks):
        self.shape = blocks.shape
        self.count = lax.axis_size("wide")
        me = lax.axis_index("wide")
        self.moved = []
        for step in range(self.count):
            block = lax.dynamic_slice_in_dim(blocks, (me + step) % self.count, 1, 0)
            if step:
                pairs = [(i, (i + step) % self.count) for i in range(self.count)]
                block = lax.ppermute(block, "wide", pairs)
            self.moved.append(block)

    def before(self, *values):
        half = self.count // 2
        self.moved[:half], values = split_tie(self.moved[:half], values)
        return values

    def join(self):
        me = lax.axis_index("wide")
        whole = jnp.zeros(self.shape, self.moved[0].dtype)
        for step, block in enumerate(self.moved):
            place = (me - step) % self.count
            whole = lax.dynamic_update_slice_in_dim(whole, block, place, 0)
        return whole


def wide_gather(shard):
    return lax.all_gather(shard, "wide", axis=0, tiled=True)


def wide_scatter(whole):
    return lax.psum_scatter(whole, "wide", scatter_dimension=0, tiled=True)


def tie(*values):
    return lax.optimization_barrier(values)


def split_tie(first, second):
    values = list(tie(*first, *second))
    return values[: len(first)], values[len(first) :]


def chip_pairs(move):
    pairs = []
    for at in range(lax.axis_size("wide")):
        target = move(at // 2, at % 2)
        if target is not None:
            pairs.append((at, target[0] * 2 + target[1]))
    return pairs


def core_swap(value):
    return lax.ppermute(value, "wide", chip_pairs(lambda chip, core: (chip, 1 - core)))


def rotated(value, same, ahead, behind):
    width = value.shape[1]
    return (
        value * same
        + pltpu.roll(value, width - HALF_ROT, 1) * ahead
        + pltpu.roll(value, HALF_ROT, 1) * behind
    )


def unrotated(value, same, ahead, behind):
    width = value.shape[1]
    return value * same - (
        pltpu.roll(value, width - HALF_ROT, 1) * ahead
        + pltpu.roll(value, HALF_ROT, 1) * behind
    )


def wide_tables(width, *refs):
    return [jnp.concatenate([ref[...]] * (width // ref.shape[1]), 1) for ref in refs]


def tables_body(col_ref, row_ref, same_ref, ahead_ref, behind_ref):
    tokens, lanes = same_ref.shape
    col = col_ref[...]
    before = jnp.zeros((tokens, 1), jnp.int32)
    for first in range(0, tokens, TOKEN_BLOCK):
        smaller = row_ref[:, first : first + TOKEN_BLOCK] < col
        before += jnp.sum(jnp.where(smaller, 1, 0), axis=1, keepdims=True)
    positions = lax.broadcasted_iota(jnp.int32, (tokens, 1), 0) - before
    dim = lax.broadcasted_iota(jnp.int32, (1, lanes), 1) % HEAD_DIM
    frequency = jnp.exp((dim % HALF_ROT).astype(F) * (-2.0 * math.log(ROPE_BASE) / ROT_DIMS))
    angles = positions.astype(F) * frequency
    cosine, sine = jnp.cos(angles), jnp.sin(angles)
    same_ref[...] = jnp.where(dim < ROT_DIMS, cosine, 1.0)
    ahead_ref[...] = jnp.where(dim < HALF_ROT, -sine, 0.0)
    behind_ref[...] = jnp.where((dim >= HALF_ROT) & (dim < ROT_DIMS), sine, 0.0)


def rotary_tables(seg_col, seg_line):
    tokens = seg_col.shape[0]
    return pl.pallas_call(
        tables_body,
        out_shape=[jax.ShapeDtypeStruct((tokens, 2 * HEAD_DIM), F)] * 3,
        name="tables",
    )(seg_col, seg_line)


def unit_rows(tensor):
    center = tensor - jnp.mean(tensor, axis=-1, keepdims=True)
    inverse = lax.rsqrt(jnp.mean(center * center, axis=-1, keepdims=True) + NORM_EPS)
    return center * inverse, inverse


def cost(products, values):
    return pl.CostEstimate(flops=2 * products, transcendentals=0, bytes_accessed=values)


def project_body(pieces, depth, norm_size, *refs):
    place_ref, x_ref, same_ref, ahead_ref, behind_ref = refs[:5]
    w_refs = refs[5 : 5 + pieces]
    q_ref, k_ref, v_ref, hat_ref, w_ref, norms_ref, bias_ref = refs[5 + pieces :]

    @pl.when(pl.program_id(0) == 0)
    def _():
        bias_ref[...] = jnp.zeros_like(bias_ref)
        for at, piece in enumerate(w_refs):
            blocks = piece.shape[0]
            rows = pl.multiple_of(place_ref[at] * depth, blocks * depth)
            columns = pl.multiple_of(place_ref[at] * norm_size, blocks * norm_size)
            for block in range(blocks):
                w_ref[pl.ds(rows + block * depth, depth), :] = piece[block, :depth]
                bias_ref[...] += piece[block, depth + 4 : depth + 5].astype(F)
            norms = [piece[block, depth : depth + 4, :norm_size].astype(F) for block in range(blocks)]
            norms_ref[:, pl.ds(columns, blocks * norm_size)] = jnp.concatenate(norms, 1)

    hat, _ = unit_rows(x_ref[...].astype(F))
    normed = (hat * norms_ref[0:1, :] + norms_ref[1:2, :]).astype(B)
    hat_ref[...] = hat.astype(B)
    out = jnp.dot(normed, w_ref[...], preferred_element_type=F) + bias_ref[...]
    width = q_ref.shape[1]
    tables = wide_tables(width, same_ref, ahead_ref, behind_ref)
    q_ref[...] = rotated(out[:, :width], *tables).astype(B)
    k_ref[...] = rotated(out[:, width : 2 * width], *tables).astype(B)
    v_ref[...] = out[:, 2 * width :].astype(B)


def row_spec(width, block):
    return pl.BlockSpec((block, width), lambda i: (i, 0))


def whole_spec(array):
    return pl.BlockSpec(array.shape, lambda i: (0, 0))


def project(x_all, gathered, tables, depth, norm_size):
    tokens, features = x_all.shape
    pieces, places = gathered.pieces()
    columns = pieces[0].shape[2]
    width = columns // 3
    block = min(TOKEN_BLOCK, tokens)
    row = lambda size: pl.BlockSpec((block, size), lambda i, place: (i, 0))
    flat = lambda *shape: pl.BlockSpec(shape, lambda i, place: (0,) * len(shape))
    return pl.pallas_call(
        functools.partial(project_body, len(pieces), depth, norm_size),
        grid_spec=pltpu.PrefetchScalarGridSpec(
            num_scalar_prefetch=1,
            grid=(tokens // block,),
            in_specs=[row(features)]
            + [row(table.shape[1]) for table in tables]
            + [flat(*piece.shape) for piece in pieces],
            out_specs=[row(width)] * 3
            + [row(features), flat(features, columns), flat(4, features), flat(1, columns)],
        ),
        out_shape=[jax.ShapeDtypeStruct((tokens, width), B)] * 3
        + [
            jax.ShapeDtypeStruct((tokens, features), B),
            jax.ShapeDtypeStruct((features, columns), B),
            jax.ShapeDtypeStruct((4, features), F),
            jax.ShapeDtypeStruct((1, columns), F),
        ],
        name="project",
        cost_estimate=cost(tokens * features * columns, 4 * tokens * features),
    )(jnp.stack(places), x_all, *tables, *pieces)


def gate_body(pieces, *refs):
    place_ref, tokens_ref = refs[:2]
    gate_ref, up_ref, hidden_ref = refs[2 + 2 * pieces :]
    sums = []
    for half in range(2):
        total = jnp.zeros(gate_ref.shape, F)
        for at in range(pieces):
            w_ref = refs[2 + half * pieces + at]
            size = w_ref.shape[1]
            columns = pl.ds(pl.multiple_of(place_ref[at], size), size)
            total += dotg(tokens_ref[:, columns], w_ref[...], NT)
        sums.append(total)
    gate_ref[...] = sums[0]
    up_ref[...] = sums[1]
    hidden_ref[...] = (sums[0] * jax.nn.sigmoid(sums[0]) * sums[1]).astype(B)


def piece_call(body, name, places, blocked, pieces, outs, products):
    tokens = blocked[0].shape[0]
    block = min(FEED_BLOCK, tokens)

    def spec(shape):
        if len(shape) == 3:
            return pl.BlockSpec((shape[0], block, shape[2]), lambda i, place: (0, i, 0))
        return pl.BlockSpec((block, shape[1]), lambda i, place: (i, 0))

    size = sum(array.size * array.dtype.itemsize for array in blocked + pieces)
    return pl.pallas_call(
        functools.partial(body, len(places)),
        grid_spec=pltpu.PrefetchScalarGridSpec(
            num_scalar_prefetch=1,
            grid=(tokens // block,),
            in_specs=[spec(array.shape) for array in blocked]
            + [pl.BlockSpec(piece.shape, lambda i, place: (0, 0)) for piece in pieces],
            out_specs=[spec(out.shape) for out in outs],
        ),
        out_shape=outs,
        name=name,
        cost_estimate=cost(products, size),
    )(jnp.stack(places), *blocked, *pieces)


def gate_up_forward(tokens_all, gate, up):
    tokens = tokens_all.shape[0]
    gates, places = gate.pieces()
    ups, _ = up.pieces()
    units = gates[0].shape[0]
    outs = [jax.ShapeDtypeStruct((tokens, units), kind) for kind in (F, F, B)]
    products = 2 * tokens * units * tokens_all.shape[1]
    return piece_call(gate_body, "gate_up", places, [tokens_all], gates + ups, outs, products)


def down_body(pieces, *refs):
    place_ref, hidden_ref = refs[:2]
    out_ref = refs[2 + pieces]
    for at in range(pieces):
        w_ref = refs[2 + at]
        size = w_ref.shape[1]
        columns = pl.ds(pl.multiple_of(place_ref[at], size), size)
        out_ref[:, columns] = jnp.dot(
            hidden_ref[...], w_ref[...], preferred_element_type=F
        ).astype(B)


def down_forward(hidden, down, features):
    tokens, units = hidden.shape
    downs, places = down.pieces()
    outs = [jax.ShapeDtypeStruct((tokens, features), B)]
    return piece_call(
        down_body, "down", places, [hidden], downs, outs, tokens * units * features
    )[0]


def feed_back_body(pieces, *refs):
    place_ref, grads_ref, gate_ref, up_ref = refs[:4]
    weights = refs[4 : 4 + 3 * pieces]
    out_ref, e_ref = refs[4 + 3 * pieces :]
    grad_hidden = jnp.zeros(gate_ref.shape, F)
    for at in range(pieces):
        size = weights[at].shape[1]
        columns = pl.ds(pl.multiple_of(place_ref[at], size), size)
        grad_hidden += dotg(grads_ref[:, columns], weights[at][...], NT)
    gate = gate_ref[...]
    sigmoid = jax.nn.sigmoid(gate)
    grad_gate = grad_hidden * up_ref[...] * sigmoid * (1.0 + gate * (1.0 - sigmoid))
    grad_gate = grad_gate.astype(B)
    grad_up = (grad_hidden * (gate * sigmoid)).astype(B)
    out_ref[0] = grad_gate
    out_ref[1] = grad_up
    for at in range(pieces):
        size = weights[at].shape[1]
        columns = pl.ds(pl.multiple_of(place_ref[at], size), size)
        e = jnp.dot(grad_gate, weights[pieces + at][...], preferred_element_type=F)
        e += jnp.dot(grad_up, weights[2 * pieces + at][...], preferred_element_type=F)
        e_ref[:, columns] = e.astype(B)


def feed_back(grads_all, gate_part, up_part, down, gate, up):
    tokens, features = grads_all.shape
    units = gate_part.shape[1]
    downs, places = down.pieces()
    outs = [
        jax.ShapeDtypeStruct((2, tokens, units), B),
        jax.ShapeDtypeStruct((tokens, features), B),
    ]
    weights = downs + gate.pieces()[0] + up.pieces()[0]
    return piece_call(
        feed_back_body,
        "feed_back",
        places,
        [grads_all, gate_part, up_part],
        weights,
        outs,
        3 * tokens * units * features,
    )


def pair_bias(seg_col, seg_row, first, size, keys):
    same = seg_col[first : first + size, :] == seg_row[:, :keys]
    key_pos = lax.broadcasted_iota(jnp.int32, (size, keys), 1)
    query_pos = first + lax.broadcasted_iota(jnp.int32, (size, keys), 0)
    return jnp.where(same & (key_pos <= query_pos), 0.0, NEG_LARGE)


def head_masks(heads, width):
    lane = lax.broadcasted_iota(jnp.int32, (1, width), 1) // HEAD_DIM
    return [jnp.where(lane == head, 1.0, 0.0).astype(B) for head in range(heads)]


def attend_body(heads, q_ref, k_ref, v_ref, seg_col, seg_row, out_ref, lse_ref):
    tokens, width = q_ref.shape
    block = min(TOKEN_BLOCK, tokens)
    masks = head_masks(heads, width)
    for first in range(0, tokens, block):
        keys = first + block
        bias = pair_bias(seg_col, seg_row, first, block, keys)
        queries = q_ref[first:keys, :]
        total = jnp.zeros((block, width), F)
        for head in range(heads):
            scores = dotg(queries * (masks[head] * SCORE_SCALE), k_ref[:keys, :], NT) + bias
            top = jnp.max(scores, axis=-1, keepdims=True)
            weights = jnp.exp(scores - top)
            norm = jnp.sum(weights, axis=-1, keepdims=True)
            probs = (weights * (1.0 / norm)).astype(B)
            total += jnp.dot(probs, v_ref[:keys, :] * masks[head], preferred_element_type=F)
            lse_ref[first:keys, head : head + 1] = top + jnp.log(norm)
        out_ref[first:keys, :] = total.astype(B)


def attend(q, k, v, seg_col, seg_row, heads):
    tokens, width = q.shape
    return pl.pallas_call(
        functools.partial(attend_body, heads),
        out_shape=[
            jax.ShapeDtypeStruct((tokens, width), B),
            jax.ShapeDtypeStruct((tokens, 128), F),
        ],
        name="attend",
        cost_estimate=cost(heads * tokens * tokens * 512, 8 * tokens * width),
    )(q, k, v, seg_col, seg_row)


def out_project_body(pieces, *refs):
    at_ref, place_ref, attended_ref, x_ref, norm_ref = refs[:5]
    piece_refs = (refs[5 : 5 + pieces], refs[5 + pieces : 5 + 2 * pieces])
    normed_ref, after_ref, mine_ref, w_ref = refs[5 + 2 * pieces :]
    core = at_ref[0]
    _, chips, width, features = w_ref.shape

    @pl.when(pl.program_id(0) == 0)
    def _():
        for same, group in enumerate(piece_refs):
            for at, piece in enumerate(group):
                place = place_ref[at]
                whole = group[0].shape[0]
                size = width * whole // (chips * width) if pieces == 1 else whole // chips
                held = piece.shape[0] // size
                slot = place // whole
                first = place % whole // size
                for chip in range(held):
                    rows = pl.ds(pl.multiple_of(slot * size, size), size)
                    w_ref[same, first + chip, rows, :] = piece[chip * size : (chip + 1) * size]
        mine_ref[...] = w_ref[0, at_ref[1]]

    total = x_ref[...].astype(F)
    for chip in range(chips):
        for same, which in enumerate((core, 1 - core)):
            total += jnp.dot(
                attended_ref[chip * 2 + which], w_ref[same, chip], preferred_element_type=F
            )
    after_ref[...] = total
    hat, _ = unit_rows(total)
    normed_ref[...] = (hat * norm_ref[0:1, :] + norm_ref[1:2, :]).astype(B)


def out_project(at, attended_all, same, other, places, x_all, norm_two):
    owners, tokens, width = attended_all.shape
    features = x_all.shape[1]
    block = min(TOKEN_BLOCK, tokens)
    flat = lambda array: pl.BlockSpec(array.shape, lambda i, at, place: (0, 0))
    rows = pl.BlockSpec((block, features), lambda i, at, place: (i, 0))
    return pl.pallas_call(
        functools.partial(out_project_body, len(same)),
        grid_spec=pltpu.PrefetchScalarGridSpec(
            num_scalar_prefetch=2,
            grid=(tokens // block,),
            in_specs=[
                pl.BlockSpec((owners, block, width), lambda i, at, place: (0, i, 0)),
                rows,
                flat(norm_two),
            ]
            + [flat(piece) for piece in same + other],
            out_specs=[
                rows,
                rows,
                pl.BlockSpec((width, features), lambda i, at, place: (0, 0)),
            ],
            scratch_shapes=[pltpu.VMEM((2, owners // 2, width, features), B)],
        ),
        out_shape=[
            jax.ShapeDtypeStruct((tokens, features), B),
            jax.ShapeDtypeStruct((tokens, features), F),
            jax.ShapeDtypeStruct((width, features), B),
        ],
        name="out_project",
        cost_estimate=cost(tokens * features * features, 8 * tokens * features),
    )(
        jnp.stack(at).astype(jnp.int32),
        jnp.stack(places).astype(jnp.int32),
        attended_all,
        x_all,
        norm_two,
        *same,
        *other,
    )


def attend_back_body(
    heads, q_ref, k_ref, v_ref, g_ref, lse_ref, seg_col, seg_row, same_ref, ahead_ref, behind_ref,
    out_ref, bias_ref, dq_ref, dk_ref, dv_ref,
):
    tokens, width = q_ref.shape
    block = min(TOKEN_BLOCK, tokens)
    masks = head_masks(heads, width)
    for first in reversed(range(0, tokens, block)):
        keys = first + block
        bias = pair_bias(seg_col, seg_row, first, block, keys)
        queries = q_ref[first:keys, :]
        grads = g_ref[first:keys, :]
        dq = jnp.zeros((block, width), F)
        stacks = ([], [], [], [])
        for head in range(heads):
            q_head = queries * (masks[head] * SCORE_SCALE)
            g_head = grads * masks[head]
            scores = dotg(q_head, k_ref[:keys, :], NT) + bias
            probs = jnp.exp(scores - lse_ref[first:keys, head : head + 1])
            weighted = probs * dotg(g_head, v_ref[:keys, :], NT)
            delta = jnp.sum(weighted, axis=-1, keepdims=True)
            grad_scores = (weighted - probs * delta).astype(B)
            dq += jnp.dot(grad_scores, k_ref[:keys, :] * masks[head], preferred_element_type=F)
            for stack, value in zip(stacks, (grad_scores, q_head, probs.astype(B), g_head)):
                stack.append(value)
        joined = [jnp.concatenate(stack, 0) for stack in stacks]
        dk = dotg(joined[0], joined[1], TN)
        dv = dotg(joined[2], joined[3], TN)
        if keys == tokens:
            dk_ref[...] = dk
            dv_ref[...] = dv
        else:
            dk_ref[:keys, :] += dk
            dv_ref[:keys, :] += dv
        dq_ref[first:keys, :] = dq * SCORE_SCALE
    tables = wide_tables(width, same_ref, ahead_ref, behind_ref)
    pieces = (unrotated(dq_ref[...], *tables), unrotated(dk_ref[...], *tables), dv_ref[...])
    for at, piece in enumerate(pieces):
        rounded = piece.astype(B)
        out_ref[:, at * width : (at + 1) * width] = rounded
        bias_ref[:, at * width : (at + 1) * width] = jnp.sum(
            rounded.astype(F), axis=0, keepdims=True
        )


def attend_back(q, k, v, grads, lse, seg_col, seg_row, tables, heads):
    tokens, width = q.shape
    return pl.pallas_call(
        functools.partial(attend_back_body, heads),
        out_shape=[
            jax.ShapeDtypeStruct((tokens, 3 * width), B),
            jax.ShapeDtypeStruct((1, 3 * width), F),
        ],
        scratch_shapes=[pltpu.VMEM((tokens, width), F)] * 3,
        name="attend_back",
        cost_estimate=cost(heads * tokens * tokens * 1024, 16 * tokens * width),
    )(q, k, v, grads, lse, seg_col, seg_row, *tables)


def weights_back_body(
    depth, norm_size, hat_ref, grad_ref, w_ref, norms_ref, two_ref, bias_ref, out_ref
):
    blocks, rows, columns = out_ref.shape
    product = dotg(hat_ref[...], grad_ref[...], TN)
    weights = w_ref[...].astype(F)
    bias = bias_ref[...]
    gain = jnp.sum(product * weights, axis=1, keepdims=True)
    shift = jnp.sum(weights * bias, axis=1, keepdims=True)
    lanes = lax.broadcasted_iota(jnp.int32, (gain.shape[0], 128), 1)
    ones = jnp.where(lanes == 0, gain, shift).T
    norms = jnp.concatenate([norms_ref[...]] * 2, 0).T
    product = (product * norms[:, 0:1] + norms[:, 1:2] * bias).astype(B)
    sums = jnp.concatenate([ones[:2], two_ref[...]], 0).astype(B)
    bias = bias.astype(B)
    for block in range(blocks):
        out_ref[block, :depth, :] = product[block * depth : (block + 1) * depth]
        mine = sums[:, block * norm_size : (block + 1) * norm_size]
        out_ref[block, depth:, :] = jnp.concatenate(
            [
                jnp.concatenate([mine, jnp.zeros((4, columns - norm_size), B)], 1),
                bias,
                jnp.zeros((rows - depth - 5, columns), B),
            ],
            0,
        )


def weights_back(hat_all, grad_proj, w_mine, norms, two, bias_grad, depth, norm_size):
    tokens, features = hat_all.shape
    columns = grad_proj.shape[1]
    block = min(512, features)
    flat = lambda array: pl.BlockSpec(array.shape, lambda i: (0, 0))
    across = lambda rows: pl.BlockSpec((rows, block), lambda i: (0, i))
    return pl.pallas_call(
        functools.partial(weights_back_body, depth, norm_size),
        grid=(features // block,),
        in_specs=[
            across(tokens),
            flat(grad_proj),
            row_spec(columns, block),
            across(4),
            across(2),
            flat(bias_grad),
        ],
        out_specs=pl.BlockSpec((block // depth, depth + EXTRA_ROWS, columns), lambda i: (i, 0, 0)),
        out_shape=jax.ShapeDtypeStruct((features // depth, depth + EXTRA_ROWS, columns), B),
        name="weights_back",
        cost_estimate=cost(tokens * features * columns, 4 * tokens * features),
    )(hat_all, grad_proj, w_mine, norms, two, bias_grad)


def norm_back_body(e_ref, x_ref, upstream_ref, gain_ref, grad_ref, *refs):
    hat, inverse = unit_rows(x_ref[...].astype(F))
    e = e_ref[...].astype(F)
    scaled = e * gain_ref[...]
    mean_grad = jnp.mean(scaled, axis=-1, keepdims=True)
    mean_proj = jnp.mean(scaled * hat, axis=-1, keepdims=True)
    grad = upstream_ref[...].astype(F) + inverse * (scaled - mean_grad - hat * mean_proj)
    grad_ref[...] = grad
    if refs:
        rounded_ref, sums_ref = refs
        rounded_ref[...] = grad.astype(B)
        sums = jnp.concatenate(
            [jnp.sum(e * hat, axis=0, keepdims=True), jnp.sum(e, axis=0, keepdims=True)], 0
        )

        @pl.when(pl.program_id(0) == 0)
        def _():
            sums_ref[...] = sums

        @pl.when(pl.program_id(0) != 0)
        def _():
            sums_ref[...] += sums


def norm_back(e, x, upstream, gain, more):
    tokens, features = x.shape
    outs = [jax.ShapeDtypeStruct((tokens, features), F)]
    if more:
        outs += [jax.ShapeDtypeStruct((tokens, features), B), jax.ShapeDtypeStruct((2, features), F)]
    block = min(64, tokens)
    rows = row_spec(features, block)
    sums = pl.BlockSpec((2, features), lambda i: (0, 0))
    return pl.pallas_call(
        norm_back_body,
        grid=(tokens // block,),
        in_specs=[rows, rows, rows, whole_spec(gain)],
        out_specs=[rows, rows, sums] if more else [rows],
        out_shape=outs,
        name="norm_back",
    )(e, x, upstream, gain)


def pack_body(strided, me_ref, w_ref, norm_ref, bias_ref, out_ref):
    wide, _, columns = out_ref.shape
    depth = w_ref.shape[0]
    third = w_ref.shape[1] // 3
    width = columns // 3
    me = me_ref[0]
    held = bias_ref.shape[1]
    padded = jnp.concatenate(
        [norm_ref[...], jnp.zeros((4, columns - norm_ref.shape[1]), B)], 1
    )
    for owner in range(wide):
        biases = []
        for part in range(3):
            for slot in range(width // HEAD_DIM):
                head = slot * wide + owner if strided else owner * (width // HEAD_DIM) + slot
                first = part * third + head * HEAD_DIM
                if slot % 2 == 0:
                    left = w_ref[:, first : first + HEAD_DIM]
                else:
                    to = part * width + (slot - 1) * HEAD_DIM
                    out_ref[owner, :depth, to : to + 2 * HEAD_DIM] = jnp.concatenate(
                        [left, w_ref[:, first : first + HEAD_DIM]], 1
                    )
                last = first + HEAD_DIM
                while first < last:
                    stop = min(last, (first // held + 1) * held)
                    mine = bias_ref[:, first % held : first % held + stop - first]
                    kept = jnp.where(me == first // held, mine.astype(F), 0.0)
                    biases.append(kept.astype(B))
                    first = stop
        out_ref[owner, depth:, :] = jnp.concatenate(
            [padded, jnp.concatenate(biases, 1), jnp.zeros((EXTRA_ROWS - 5, columns), B)], 0
        )


def pack(me, w_qkv, norm_params, b_qkv, strided, wide):
    depth, columns = w_qkv.shape
    memory = [pltpu.SMEM] + [pltpu.VMEM] * 3
    return pl.pallas_call(
        functools.partial(pack_body, strided),
        in_specs=[pl.BlockSpec(memory_space=space) for space in memory],
        out_shape=jax.ShapeDtypeStruct((wide, depth + EXTRA_ROWS, columns // wide), B),
        name="pack",
    )(me[None].astype(jnp.int32), w_qkv, norm_params, b_qkv[None])


def adam_step(parameter, gradient, moments):
    first_moment = BETA_ONE * moments[0] + (1.0 - BETA_ONE) * gradient
    second_moment = BETA_TWO * moments[1] + (1.0 - BETA_TWO) * gradient * gradient
    return first_moment / BIAS_FIRST / (
        jnp.sqrt(second_moment / BIAS_SECOND) + ADAM_EPS
    ) + DECAY_RATE * parameter.astype(F)


def finish_body(strided, wide, got_ref, w_ref, moment_ref, grad_ref, step_ref):
    depth, third = w_ref.shape
    width = got_ref.shape[2]
    for at in range(third // 128):
        if strided:
            slot, owner = at * 2 // wide, at * 2 % wide
            first = slot * HEAD_DIM
            gradient = jnp.concatenate(
                [got_ref[owner + k, :depth, first : first + HEAD_DIM] for k in range(2)], 1
            )
        else:
            owner, first = at * 128 // width, at * 128 % width
            gradient = got_ref[owner, :depth, first : first + 128]
        gradient = gradient.astype(F)
        columns = slice(at * 128, at * 128 + 128)
        grad_ref[:, columns] = gradient
        step_ref[:, columns] = adam_step(
            w_ref[:, columns], gradient, (moment_ref[0, :, columns], moment_ref[1, :, columns])
        )


def finish(received, w_qkv, moments, strided):
    wide, rows, columns = received.shape
    depth = w_qkv.shape[0]
    third = w_qkv.shape[1] // 3
    part = pl.BlockSpec((depth, third), lambda i: (0, i))
    return pl.pallas_call(
        functools.partial(finish_body, strided, wide),
        grid=(3,),
        in_specs=[
            pl.BlockSpec((wide, rows, columns // 3), lambda i: (0, 0, i)),
            part,
            pl.BlockSpec((2, depth, third), lambda i: (0, 0, i)),
        ],
        out_specs=[part, part],
        out_shape=[jax.ShapeDtypeStruct(w_qkv.shape, F)] * 2,
        name="finish",
    )(received, w_qkv, moments)


def shards(
    block_input, out_grad, segment_ids, positions, norm_params, w_qkv, b_qkv, w_out, gate_up, w_down,
    moment_norm, moment_qkv, moment_bias, moment_out, moment_gate, moment_down,
):
    x_own = block_input[0]
    local_len, features = x_own.shape
    rows = lax.axis_size("rows")
    wide = lax.axis_size("wide")
    my_row = lax.axis_index("rows")
    my_wide = lax.axis_index("wide")
    segment_row = segment_ids[0]
    heads = HEADS // wide
    width = heads * HEAD_DIM
    depth = w_qkv.shape[0]
    norm_size = norm_params.shape[1]
    strided = depth == HEAD_DIM

    bias_size = b_qkv.shape[0]
    chips = wide // 2
    core = my_wide % 2
    blocks = range(rows * wide)
    back = [(b % rows * wide + b // rows, b) for b in blocks]
    gate_first = gate_up.swapaxes(1, 2)
    packed = pack(my_row * wide + my_wide, w_qkv, norm_params, b_qkv, strided, wide)
    packed, gate_shard = tie(packed, gate_first[0])
    gate = RowsGather(gate_shard, 1)
    exchange = WideExchange(packed)
    segment_row, *arrived = exchange.before(segment_row, *(gate.step or ()))
    gate.step = arrived or None
    received, x_first = tie(exchange.join(), x_own)
    x_all = wide_gather(x_first)
    w_rows = RowsGather(received, 0)
    seg_col = segment_row[:, None]
    seg_line = segment_row[None, :]
    tables = w_rows.before(*rotary_tables(seg_col, seg_line))
    w_rows.second()
    if gate.step:
        up_first, *gate.step = w_rows.before(gate_first[1], *gate.step)
    else:
        up_first = gate_first[1]
    x_all, up_first = tie(gate.halves(x_all), up_first)
    up = RowsGather(up_first, 1)
    gate.second()
    if strided:
        x_all, out_first = w_rows.before(x_all, w_out)
        out_line = lax.all_gather(out_first, "wide", axis=0, tiled=False)
    q, k, v, hat_all, w_mine, norms, _ = project(x_all, w_rows, tables, depth, norm_size)
    attended, lse = attend(q, k, v, seg_col, seg_line, heads)
    attended = gate.before(up.before(attended))
    if strided:
        attended, out_line = tie(attended, out_line)
    attended_all = lax.all_gather(attended, "wide", axis=0, tiled=False)
    if strided:
        out_line = out_line.reshape(chips, 2, depth, features)
        out_line = lax.dynamic_index_in_dim(out_line, core, 1, False)
        out_rows = RowsGather(out_line.reshape(chips * depth, features), 0)
        out_rows.second()
        out_rows.step = up.before(*out_rows.step) if out_rows.step else None
        out_pieces, out_places = out_rows.pieces()
    else:
        out_all = lax.all_gather(w_out, ("rows", "wide"), axis=0, tiled=True)
        out_all = out_all.reshape(chips, 2, width, features)
        out_line = lax.dynamic_index_in_dim(out_all, core, 1, False)
        out_pieces, out_places = [out_line.reshape(chips * width, features)], [jnp.int32(0)]
    swapped = [core_swap(piece) for piece in out_pieces]
    norms_two = norms[2:]
    attended_all = up.halves(attended_all)
    up.second()
    attended_all, upstream, down_first, norms_two, *swapped = tie(
        attended_all, out_grad[0], w_down, norms_two, *swapped
    )
    down = RowsGather(down_first, 1)
    grads_all = wide_gather(upstream)
    tokens_all, after_all, out_mine = out_project(
        (core, my_wide // 2), attended_all, out_pieces, swapped, out_places, x_all, norms_two
    )
    tokens_all = down.before(tokens_all)
    down.second()
    after_attn = lax.dynamic_slice_in_dim(after_all, my_wide * local_len, local_len, 0)
    gate_part, up_part, hidden = gate_up_forward(tokens_all, gate, up)

    gate_grads, e_two = feed_back(grads_all, gate_part, up_part, down, gate, up)
    grad_normed_two = wide_scatter(e_two)
    gate_grads, hidden, tokens_all, grads_all = tie(gate_grads, hidden, tokens_all, grads_all)
    gate_grad = jnp.einsum("gtf,td->gfd", gate_grads, tokens_all, preferred_element_type=F).astype(B)
    down_grad = jnp.einsum("tf,td->fd", hidden, grads_all, preferred_element_type=F).astype(B)
    grad_down = RowsSum(down_grad, 1)
    grad_gate = RowsSum(gate_grad, 2)
    grad_normed_two = grad_gate.before(grad_down.before(grad_normed_two))
    hidden, *_ = tie(hidden, *grad_down.second(), *grad_gate.second())
    mlp_part = down_forward(hidden, down, features)

    grad_after, branch, sums_two = norm_back(
        grad_normed_two, after_attn, out_grad[0], norms[2:3], True
    )
    branch_all = wide_gather(branch)
    mlp_part, branch_all = grad_gate.after(mlp_part, branch_all)
    mlp_out = wide_scatter(mlp_part)
    grad_attended = dotg(branch_all, out_mine, NT).astype(B)
    grad_proj, bias_grad = attend_back(
        q, k, v, grad_attended, lse, seg_col, seg_line, tables, heads
    )
    grad_proj = grad_down.after(grad_proj)
    e_one = dotg(grad_proj, w_mine, NT).astype(B)
    e_one, grad_proj, branch_all = tie(e_one, grad_proj, branch_all)
    grad_normed_one = wide_scatter(e_one)
    grad_out = RowsSum(dotg(attended, branch_all, TN).astype(B), 0)
    packed = weights_back(
        hat_all, grad_proj, w_mine, norms, sums_two, bias_grad, depth, norm_size
    )
    qkv_sum = RowsSum(packed, 0)
    qkv_sum.whole = grad_out.before(qkv_sum.whole)
    grad_out.second()
    start = no_change(qkv_sum.second()[0])
    mlp_out = qkv_sum.after(mlp_out)
    exchange = WideExchange(qkv_sum.result().astype(B))
    grad_out = grad_out.result() + start
    if not strided:
        grad_out = lax.ppermute(grad_out.astype(B), ("rows", "wide"), back).astype(F)
    grad_down = grad_down.result() + start
    grad_gate = (grad_gate.result() + start).swapaxes(1, 2)
    step_out = adam_step(w_out, grad_out, moment_out)
    step_gate = adam_step(gate_up, grad_gate, moment_gate)
    step_down = adam_step(w_down, grad_down, moment_down)
    received = exchange.join()

    block_out = (after_attn + mlp_out.astype(F)).astype(B)
    grad_qkv, step_qkv = finish(received, w_qkv, moment_qkv, strided)
    grad_qkv, step_qkv, grad_normed_one = tie(grad_qkv, step_qkv, grad_normed_one)
    input_grad = norm_back(grad_normed_one, x_own, grad_after, norms[0:1], False)[0]
    extra = received[:, depth : depth + 5].astype(F)
    grad_norms = jnp.sum(extra[:, :4, :norm_size], axis=0)
    bias_all = extra[:, 4].reshape(wide, 3, heads, HEAD_DIM)
    bias_all = bias_all.transpose((1, 2, 0, 3) if strided else (1, 0, 2, 3)).reshape(-1)
    grad_bias = lax.dynamic_slice_in_dim(
        bias_all, (my_row * wide + my_wide) * bias_size, bias_size, 0
    )

    return (
        block_out[None],
        input_grad[None],
        grad_norms,
        grad_qkv,
        grad_bias,
        grad_out,
        grad_gate,
        grad_down,
        adam_step(norm_params, grad_norms, moment_norm),
        step_qkv,
        adam_step(b_qkv, grad_bias, moment_bias),
        step_out,
        step_gate,
        step_down,
    )


def solution(mesh):
    both = ("rows", "wide")
    tokens = P("rows", "wide", None)
    weights = (P(None, both), P(both, None), P(both), P(both, None), P(None, "rows", "wide"), P("wide", "rows"))
    moments = tuple(P(None, *spec) for spec in weights)
    return jax.shard_map(
        shards,
        mesh=mesh,
        in_specs=(tokens, tokens, P("rows", None), P("rows", "wide")) + weights + moments,
        out_specs=(tokens, tokens) + weights + weights,
        check_vma=False,
    )
```

```python
import functools
import math

import jax
import jax.numpy as jnp
from jax import lax
from jax.experimental import pallas as pl
from jax.experimental.pallas import tpu as pltpu
from jax.sharding import PartitionSpec as P

F = jnp.float32
B = jnp.bfloat16
HEADS = 32
HEAD_DIM = 64
ROT_DIMS = 16
HALF_ROT = ROT_DIMS // 2
NORM_EPS = 1e-05
NEG_LARGE = -1e30
SCORE_SCALE = 0.125
ROPE_BASE = 10000.0
BETA_ONE = 0.9
BETA_TWO = 0.95
BIAS_FIRST = 0.999973438601112
BIAS_SECOND = 0.994079470779667
ADAM_EPS = 1e-08
DECAY_RATE = 0.1
TOKEN_BLOCK = 256
FEED_BLOCK = 256
EXTRA_ROWS = 8
NT = (((1,), (1,)), ((), ()))
TN = (((0,), (0,)), ((), ()))


def dotg(left, right, dims):
    return lax.dot_general(left, right, dims, preferred_element_type=F)


def plus(left, right):
    return (left.astype(F) + right.astype(F)).astype(B)


def rows_swap(value, bits):
    return lax.ppermute(value, "rows", [(i, i ^ bits) for i in range(4)])


class RowsGather:
    def __init__(self, shard, axis):
        self.axis = axis
        self.size = shard.shape[axis]
        self.step = self.whole = self.sends = None
        if lax.axis_size("rows") == 4:
            self.shard = shard
            self.step = (rows_swap(shard, 1), rows_swap(shard, 2))
        else:
            self.whole = lax.all_gather(shard, "rows", axis=axis, tiled=True)

    def before(self, *values):
        if self.step is not None:
            near, far, *values = tie(*self.step, *values)
            self.step = (near, far)
        return values if len(values) > 1 else values[0]

    def after(self, *values):
        if self.step is not None:
            self.step = tie(*self.step, *values)[:2]

    def halves(self, *values):
        if self.step is not None:
            self.near, self.far = self.step
            half = self.size // 2
            first = lax.slice_in_dim(self.near, 0, half, axis=self.axis)
            last = lax.slice_in_dim(self.far, half, self.size, axis=self.axis)
            first, last, *values = tie(first, last, *values) if values else (first, last)
            self.sends = (first, last)
        return values if len(values) > 1 else values[0] if values else None

    def second(self):
        if self.step is not None:
            if self.sends is None:
                self.halves()
            self.step = (rows_swap(self.sends[0], 2), rows_swap(self.sends[1], 1))
        return self

    def pieces(self):
        if self.whole is not None:
            return [self.whole], [jnp.int32(0)]
        me = lax.axis_index("rows")
        places = [(me ^ bits) * self.size for bits in range(4)]
        arrays = [self.shard, self.near, self.far, *self.step]
        return arrays, places + [places[3] + self.size // 2]

    def join(self):
        if self.whole is not None:
            return self.whole
        shape = list(self.shard.shape)
        shape[self.axis] = 4 * self.size
        whole = jnp.zeros(shape, self.shard.dtype)
        for piece, place in zip(*self.pieces()):
            whole = lax.dynamic_update_slice_in_dim(whole, piece, place, self.axis)
        return whole


class RowsSum:
    def __init__(self, whole, axis):
        self.whole, self.axis = whole, axis
        self.arrived = self.sent = None
        if lax.axis_size("rows") == 4:
            diagonal = self.part(3)
            half = diagonal.shape[0] // 2
            self.arrived = (rows_swap(diagonal[:half], 1), rows_swap(diagonal[half:], 2))

    def part(self, bits):
        size = self.whole.shape[self.axis] // 4
        start = (lax.axis_index("rows") ^ bits) * size
        return lax.dynamic_slice_in_dim(self.whole, start, size, self.axis)

    def before(self, value):
        if self.arrived is not None:
            near, far, value = tie(*self.arrived, value)
            self.arrived = (near, far)
        return value

    def result(self):
        if self.arrived is None:
            return lax.psum_scatter(
                self.whole, "rows", scatter_dimension=self.axis, tiled=True
            ).astype(F)
        if self.sent is None:
            self.second()
        far, near = self.sent
        return self.part(0).astype(F) + far.astype(F) + near.astype(F)

    def arrived_or_whole(self):
        return (self.whole,) if self.arrived is None else self.arrived

    def second(self):
        if self.arrived is None:
            return self.whole, self.whole
        near, far = self.part(1), self.part(2)
        half = near.shape[0] // 2
        far = jnp.concatenate([plus(far[:half], self.arrived[0]), far[half:]], 0)
        near = jnp.concatenate([near[:half], plus(near[half:], self.arrived[1])], 0)
        self.sent = (rows_swap(far, 2), rows_swap(near, 1))
        return far, near

    def after(self, *values):
        if self.arrived is None:
            self.whole, *values = tie(self.whole, *values)
        else:
            far, near, *values = tie(*self.sent, *values)
            self.sent = (far, near)
        return values if len(values) > 1 else values[0]


def no_change(value):
    return jnp.minimum(jnp.abs(value[(0,) * value.ndim].astype(F)), 0.0)


class WideExchange:
    def __init__(self, blocks):
        self.shape = blocks.shape
        self.count = lax.axis_size("wide")
        me = lax.axis_index("wide")
        self.moved = []
        for step in range(self.count):
            block = lax.dynamic_slice_in_dim(blocks, (me + step) % self.count, 1, 0)
            if step:
                pairs = [(i, (i + step) % self.count) for i in range(self.count)]
                block = lax.ppermute(block, "wide", pairs)
            self.moved.append(block)

    def before(self, *values):
        half = self.count // 2
        self.moved[:half], values = split_tie(self.moved[:half], values)
        return values

    def join(self):
        me = lax.axis_index("wide")
        whole = jnp.zeros(self.shape, self.moved[0].dtype)
        for step, block in enumerate(self.moved):
            place = (me - step) % self.count
            whole = lax.dynamic_update_slice_in_dim(whole, block, place, 0)
        return whole


def wide_gather(shard):
    return lax.all_gather(shard, "wide", axis=0, tiled=True)


def wide_scatter(whole):
    return lax.psum_scatter(whole, "wide", scatter_dimension=0, tiled=True)


def tie(*values):
    return lax.optimization_barrier(values)


def split_tie(first, second):
    values = list(tie(*first, *second))
    return values[: len(first)], values[len(first) :]


def chip_pairs(move):
    pairs = []
    for at in range(lax.axis_size("wide")):
        target = move(at // 2, at % 2)
        if target is not None:
            pairs.append((at, target[0] * 2 + target[1]))
    return pairs


def core_swap(value):
    return lax.ppermute(value, "wide", chip_pairs(lambda chip, core: (chip, 1 - core)))


def rotated(value, same, ahead, behind):
    width = value.shape[1]
    return (
        value * same
        + pltpu.roll(value, width - HALF_ROT, 1) * ahead
        + pltpu.roll(value, HALF_ROT, 1) * behind
    )


def unrotated(value, same, ahead, behind):
    width = value.shape[1]
    return value * same - (
        pltpu.roll(value, width - HALF_ROT, 1) * ahead
        + pltpu.roll(value, HALF_ROT, 1) * behind
    )


def wide_tables(width, *refs):
    return [jnp.concatenate([ref[...]] * (width // ref.shape[1]), 1) for ref in refs]


def tables_body(col_ref, row_ref, same_ref, ahead_ref, behind_ref):
    tokens, lanes = same_ref.shape
    col = col_ref[...]
    before = jnp.zeros((tokens, 1), jnp.int32)
    for first in range(0, tokens, TOKEN_BLOCK):
        smaller = row_ref[:, first : first + TOKEN_BLOCK] < col
        before += jnp.sum(jnp.where(smaller, 1, 0), axis=1, keepdims=True)
    positions = lax.broadcasted_iota(jnp.int32, (tokens, 1), 0) - before
    dim = lax.broadcasted_iota(jnp.int32, (1, lanes), 1) % HEAD_DIM
    frequency = jnp.exp((dim % HALF_ROT).astype(F) * (-2.0 * math.log(ROPE_BASE) / ROT_DIMS))
    angles = positions.astype(F) * frequency
    cosine, sine = jnp.cos(angles), jnp.sin(angles)
    same_ref[...] = jnp.where(dim < ROT_DIMS, cosine, 1.0)
    ahead_ref[...] = jnp.where(dim < HALF_ROT, -sine, 0.0)
    behind_ref[...] = jnp.where((dim >= HALF_ROT) & (dim < ROT_DIMS), sine, 0.0)


def rotary_tables(seg_col, seg_line):
    tokens = seg_col.shape[0]
    return pl.pallas_call(
        tables_body,
        out_shape=[jax.ShapeDtypeStruct((tokens, 2 * HEAD_DIM), F)] * 3,
        name="tables",
    )(seg_col, seg_line)


def unit_rows(tensor):
    center = tensor - jnp.mean(tensor, axis=-1, keepdims=True)
    inverse = lax.rsqrt(jnp.mean(center * center, axis=-1, keepdims=True) + NORM_EPS)
    return center * inverse, inverse


def cost(products, values):
    return pl.CostEstimate(flops=2 * products, transcendentals=0, bytes_accessed=values)


def project_body(pieces, depth, norm_size, *refs):
    place_ref, x_ref, same_ref, ahead_ref, behind_ref = refs[:5]
    w_refs = refs[5 : 5 + pieces]
    q_ref, k_ref, v_ref, hat_ref, w_ref, norms_ref, bias_ref = refs[5 + pieces :]

    @pl.when(pl.program_id(0) == 0)
    def _():
        bias_ref[...] = jnp.zeros_like(bias_ref)
        for at, piece in enumerate(w_refs):
            blocks = piece.shape[0]
            rows = pl.multiple_of(place_ref[at] * depth, blocks * depth)
            columns = pl.multiple_of(place_ref[at] * norm_size, blocks * norm_size)
            for block in range(blocks):
                w_ref[pl.ds(rows + block * depth, depth), :] = piece[block, :depth]
                bias_ref[...] += piece[block, depth + 4 : depth + 5].astype(F)
            norms = [piece[block, depth : depth + 4, :norm_size].astype(F) for block in range(blocks)]
            norms_ref[:, pl.ds(columns, blocks * norm_size)] = jnp.concatenate(norms, 1)

    hat, _ = unit_rows(x_ref[...].astype(F))
    normed = (hat * norms_ref[0:1, :] + norms_ref[1:2, :]).astype(B)
    hat_ref[...] = hat.astype(B)
    out = jnp.dot(normed, w_ref[...], preferred_element_type=F) + bias_ref[...]
    width = q_ref.shape[1]
    tables = wide_tables(width, same_ref, ahead_ref, behind_ref)
    q_ref[...] = rotated(out[:, :width], *tables).astype(B)
    k_ref[...] = rotated(out[:, width : 2 * width], *tables).astype(B)
    v_ref[...] = out[:, 2 * width :].astype(B)


def row_spec(width, block):
    return pl.BlockSpec((block, width), lambda i: (i, 0))


def whole_spec(array):
    return pl.BlockSpec(array.shape, lambda i: (0, 0))


def project(x_all, gathered, tables, depth, norm_size):
    tokens, features = x_all.shape
    pieces, places = gathered.pieces()
    columns = pieces[0].shape[2]
    width = columns // 3
    block = min(TOKEN_BLOCK, tokens)
    row = lambda size: pl.BlockSpec((block, size), lambda i, place: (i, 0))
    flat = lambda *shape: pl.BlockSpec(shape, lambda i, place: (0,) * len(shape))
    return pl.pallas_call(
        functools.partial(project_body, len(pieces), depth, norm_size),
        grid_spec=pltpu.PrefetchScalarGridSpec(
            num_scalar_prefetch=1,
            grid=(tokens // block,),
            in_specs=[row(features)]
            + [row(table.shape[1]) for table in tables]
            + [flat(*piece.shape) for piece in pieces],
            out_specs=[row(width)] * 3
            + [row(features), flat(features, columns), flat(4, features), flat(1, columns)],
        ),
        out_shape=[jax.ShapeDtypeStruct((tokens, width), B)] * 3
        + [
            jax.ShapeDtypeStruct((tokens, features), B),
            jax.ShapeDtypeStruct((features, columns), B),
            jax.ShapeDtypeStruct((4, features), F),
            jax.ShapeDtypeStruct((1, columns), F),
        ],
        name="project",
        cost_estimate=cost(tokens * features * columns, 4 * tokens * features),
    )(jnp.stack(places), x_all, *tables, *pieces)


def gate_body(pieces, *refs):
    place_ref, tokens_ref = refs[:2]
    gate_ref, up_ref, hidden_ref = refs[2 + 2 * pieces :]
    sums = []
    for half in range(2):
        total = jnp.zeros(gate_ref.shape, F)
        for at in range(pieces):
            w_ref = refs[2 + half * pieces + at]
            size = w_ref.shape[1]
            columns = pl.ds(pl.multiple_of(place_ref[at], size), size)
            total += dotg(tokens_ref[:, columns], w_ref[...], NT)
        sums.append(total)
    gate_ref[...] = sums[0]
    up_ref[...] = sums[1]
    hidden_ref[...] = (sums[0] * jax.nn.sigmoid(sums[0]) * sums[1]).astype(B)


def piece_call(body, name, places, blocked, pieces, outs, products):
    tokens = blocked[0].shape[0]
    block = min(FEED_BLOCK, tokens)

    def spec(shape):
        if len(shape) == 3:
            return pl.BlockSpec((shape[0], block, shape[2]), lambda i, place: (0, i, 0))
        return pl.BlockSpec((block, shape[1]), lambda i, place: (i, 0))

    size = sum(array.size * array.dtype.itemsize for array in blocked + pieces)
    return pl.pallas_call(
        functools.partial(body, len(places)),
        grid_spec=pltpu.PrefetchScalarGridSpec(
            num_scalar_prefetch=1,
            grid=(tokens // block,),
            in_specs=[spec(array.shape) for array in blocked]
            + [pl.BlockSpec(piece.shape, lambda i, place: (0, 0)) for piece in pieces],
            out_specs=[spec(out.shape) for out in outs],
        ),
        out_shape=outs,
        name=name,
        cost_estimate=cost(products, size),
    )(jnp.stack(places), *blocked, *pieces)


def gate_up_forward(tokens_all, gate, up):
    tokens = tokens_all.shape[0]
    gates, places = gate.pieces()
    ups, _ = up.pieces()
    units = gates[0].shape[0]
    outs = [jax.ShapeDtypeStruct((tokens, units), kind) for kind in (F, F, B)]
    products = 2 * tokens * units * tokens_all.shape[1]
    return piece_call(gate_body, "gate_up", places, [tokens_all], gates + ups, outs, products)


def down_body(pieces, *refs):
    place_ref, hidden_ref = refs[:2]
    out_ref = refs[2 + pieces]
    for at in range(pieces):
        w_ref = refs[2 + at]
        size = w_ref.shape[1]
        columns = pl.ds(pl.multiple_of(place_ref[at], size), size)
        out_ref[:, columns] = jnp.dot(
            hidden_ref[...], w_ref[...], preferred_element_type=F
        ).astype(B)


def down_forward(hidden, down, features):
    tokens, units = hidden.shape
    downs, places = down.pieces()
    outs = [jax.ShapeDtypeStruct((tokens, features), B)]
    return piece_call(
        down_body, "down", places, [hidden], downs, outs, tokens * units * features
    )[0]


def feed_back_body(pieces, *refs):
    place_ref, grads_ref, gate_ref, up_ref = refs[:4]
    weights = refs[4 : 4 + 3 * pieces]
    out_ref, e_ref = refs[4 + 3 * pieces :]
    grad_hidden = jnp.zeros(gate_ref.shape, F)
    for at in range(pieces):
        size = weights[at].shape[1]
        columns = pl.ds(pl.multiple_of(place_ref[at], size), size)
        grad_hidden += dotg(grads_ref[:, columns], weights[at][...], NT)
    gate = gate_ref[...]
    sigmoid = jax.nn.sigmoid(gate)
    grad_gate = grad_hidden * up_ref[...] * sigmoid * (1.0 + gate * (1.0 - sigmoid))
    grad_gate = grad_gate.astype(B)
    grad_up = (grad_hidden * (gate * sigmoid)).astype(B)
    out_ref[0] = grad_gate
    out_ref[1] = grad_up
    for at in range(pieces):
        size = weights[at].shape[1]
        columns = pl.ds(pl.multiple_of(place_ref[at], size), size)
        e = jnp.dot(grad_gate, weights[pieces + at][...], preferred_element_type=F)
        e += jnp.dot(grad_up, weights[2 * pieces + at][...], preferred_element_type=F)
        e_ref[:, columns] = e.astype(B)


def feed_back(grads_all, gate_part, up_part, down, gate, up):
    tokens, features = grads_all.shape
    units = gate_part.shape[1]
    downs, places = down.pieces()
    outs = [
        jax.ShapeDtypeStruct((2, tokens, units), B),
        jax.ShapeDtypeStruct((tokens, features), B),
    ]
    weights = downs + gate.pieces()[0] + up.pieces()[0]
    return piece_call(
        feed_back_body,
        "feed_back",
        places,
        [grads_all, gate_part, up_part],
        weights,
        outs,
        3 * tokens * units * features,
    )


def pair_bias(seg_col, seg_row, first, size, keys):
    same = seg_col[first : first + size, :] == seg_row[:, :keys]
    key_pos = lax.broadcasted_iota(jnp.int32, (size, keys), 1)
    query_pos = first + lax.broadcasted_iota(jnp.int32, (size, keys), 0)
    return jnp.where(same & (key_pos <= query_pos), 0.0, NEG_LARGE)


def head_masks(heads, width):
    lane = lax.broadcasted_iota(jnp.int32, (1, width), 1) // HEAD_DIM
    return [jnp.where(lane == head, 1.0, 0.0).astype(B) for head in range(heads)]


def attend_body(heads, q_ref, k_ref, v_ref, seg_col, seg_row, out_ref, lse_ref):
    tokens, width = q_ref.shape
    block = min(TOKEN_BLOCK, tokens)
    masks = head_masks(heads, width)
    for first in range(0, tokens, block):
        keys = first + block
        bias = pair_bias(seg_col, seg_row, first, block, keys)
        queries = q_ref[first:keys, :]
        total = jnp.zeros((block, width), F)
        for head in range(heads):
            scores = dotg(queries * (masks[head] * SCORE_SCALE), k_ref[:keys, :], NT) + bias
            top = jnp.max(scores, axis=-1, keepdims=True)
            weights = jnp.exp(scores - top)
            norm = jnp.sum(weights, axis=-1, keepdims=True)
            probs = (weights * (1.0 / norm)).astype(B)
            total += jnp.dot(probs, v_ref[:keys, :] * masks[head], preferred_element_type=F)
            lse_ref[first:keys, head : head + 1] = top + jnp.log(norm)
        out_ref[first:keys, :] = total.astype(B)


def attend(q, k, v, seg_col, seg_row, heads):
    tokens, width = q.shape
    return pl.pallas_call(
        functools.partial(attend_body, heads),
        out_shape=[
            jax.ShapeDtypeStruct((tokens, width), B),
            jax.ShapeDtypeStruct((tokens, 128), F),
        ],
        name="attend",
        cost_estimate=cost(heads * tokens * tokens * 512, 8 * tokens * width),
    )(q, k, v, seg_col, seg_row)


def out_project_body(pieces, *refs):
    at_ref, place_ref, attended_ref, x_ref, norm_ref = refs[:5]
    piece_refs = (refs[5 : 5 + pieces], refs[5 + pieces : 5 + 2 * pieces])
    normed_ref, after_ref, mine_ref, w_ref = refs[5 + 2 * pieces :]
    core = at_ref[0]
    _, chips, width, features = w_ref.shape

    @pl.when(pl.program_id(0) == 0)
    def _():
        for same, group in enumerate(piece_refs):
            for at, piece in enumerate(group):
                place = place_ref[at]
                whole = group[0].shape[0]
                size = width * whole // (chips * width) if pieces == 1 else whole // chips
                held = piece.shape[0] // size
                slot = place // whole
                first = place % whole // size
                for chip in range(held):
                    rows = pl.ds(pl.multiple_of(slot * size, size), size)
                    w_ref[same, first + chip, rows, :] = piece[chip * size : (chip + 1) * size]
        mine_ref[...] = w_ref[0, at_ref[1]]

    total = x_ref[...].astype(F)
    for chip in range(chips):
        for same, which in enumerate((core, 1 - core)):
            total += jnp.dot(
                attended_ref[chip * 2 + which], w_ref[same, chip], preferred_element_type=F
            )
    after_ref[...] = total
    hat, _ = unit_rows(total)
    normed_ref[...] = (hat * norm_ref[0:1, :] + norm_ref[1:2, :]).astype(B)


def out_project(at, attended_all, same, other, places, x_all, norm_two):
    owners, tokens, width = attended_all.shape
    features = x_all.shape[1]
    block = min(TOKEN_BLOCK, tokens)
    flat = lambda array: pl.BlockSpec(array.shape, lambda i, at, place: (0, 0))
    rows = pl.BlockSpec((block, features), lambda i, at, place: (i, 0))
    return pl.pallas_call(
        functools.partial(out_project_body, len(same)),
        grid_spec=pltpu.PrefetchScalarGridSpec(
            num_scalar_prefetch=2,
            grid=(tokens // block,),
            in_specs=[
                pl.BlockSpec((owners, block, width), lambda i, at, place: (0, i, 0)),
                rows,
                flat(norm_two),
            ]
            + [flat(piece) for piece in same + other],
            out_specs=[
                rows,
                rows,
                pl.BlockSpec((width, features), lambda i, at, place: (0, 0)),
            ],
            scratch_shapes=[pltpu.VMEM((2, owners // 2, width, features), B)],
        ),
        out_shape=[
            jax.ShapeDtypeStruct((tokens, features), B),
            jax.ShapeDtypeStruct((tokens, features), F),
            jax.ShapeDtypeStruct((width, features), B),
        ],
        name="out_project",
        cost_estimate=cost(tokens * features * features, 8 * tokens * features),
    )(
        jnp.stack(at).astype(jnp.int32),
        jnp.stack(places).astype(jnp.int32),
        attended_all,
        x_all,
        norm_two,
        *same,
        *other,
    )


def attend_back_body(
    heads, q_ref, k_ref, v_ref, g_ref, lse_ref, seg_col, seg_row, same_ref, ahead_ref, behind_ref,
    out_ref, bias_ref, dq_ref, dk_ref, dv_ref,
):
    tokens, width = q_ref.shape
    block = min(TOKEN_BLOCK, tokens)
    masks = head_masks(heads, width)
    for first in reversed(range(0, tokens, block)):
        keys = first + block
        bias = pair_bias(seg_col, seg_row, first, block, keys)
        queries = q_ref[first:keys, :]
        grads = g_ref[first:keys, :]
        dq = jnp.zeros((block, width), F)
        stacks = ([], [], [], [])
        for head in range(heads):
            q_head = queries * (masks[head] * SCORE_SCALE)
            g_head = grads * masks[head]
            scores = dotg(q_head, k_ref[:keys, :], NT) + bias
            probs = jnp.exp(scores - lse_ref[first:keys, head : head + 1])
            weighted = probs * dotg(g_head, v_ref[:keys, :], NT)
            delta = jnp.sum(weighted, axis=-1, keepdims=True)
            grad_scores = (weighted - probs * delta).astype(B)
            dq += jnp.dot(grad_scores, k_ref[:keys, :] * masks[head], preferred_element_type=F)
            for stack, value in zip(stacks, (grad_scores, q_head, probs.astype(B), g_head)):
                stack.append(value)
        joined = [jnp.concatenate(stack, 0) for stack in stacks]
        dk = dotg(joined[0], joined[1], TN)
        dv = dotg(joined[2], joined[3], TN)
        if keys == tokens:
            dk_ref[...] = dk
            dv_ref[...] = dv
        else:
            dk_ref[:keys, :] += dk
            dv_ref[:keys, :] += dv
        dq_ref[first:keys, :] = dq * SCORE_SCALE
    tables = wide_tables(width, same_ref, ahead_ref, behind_ref)
    pieces = (unrotated(dq_ref[...], *tables), unrotated(dk_ref[...], *tables), dv_ref[...])
    for at, piece in enumerate(pieces):
        rounded = piece.astype(B)
        out_ref[:, at * width : (at + 1) * width] = rounded
        bias_ref[:, at * width : (at + 1) * width] = jnp.sum(
            rounded.astype(F), axis=0, keepdims=True
        )


def attend_back(q, k, v, grads, lse, seg_col, seg_row, tables, heads):
    tokens, width = q.shape
    return pl.pallas_call(
        functools.partial(attend_back_body, heads),
        out_shape=[
            jax.ShapeDtypeStruct((tokens, 3 * width), B),
            jax.ShapeDtypeStruct((1, 3 * width), F),
        ],
        scratch_shapes=[pltpu.VMEM((tokens, width), F)] * 3,
        name="attend_back",
        cost_estimate=cost(heads * tokens * tokens * 1024, 16 * tokens * width),
    )(q, k, v, grads, lse, seg_col, seg_row, *tables)


def weights_back_body(
    depth, norm_size, hat_ref, grad_ref, w_ref, norms_ref, two_ref, bias_ref, out_ref
):
    blocks, rows, columns = out_ref.shape
    product = dotg(hat_ref[...], grad_ref[...], TN)
    weights = w_ref[...].astype(F)
    bias = bias_ref[...]
    gain = jnp.sum(product * weights, axis=1, keepdims=True)
    shift = jnp.sum(weights * bias, axis=1, keepdims=True)
    lanes = lax.broadcasted_iota(jnp.int32, (gain.shape[0], 128), 1)
    ones = jnp.where(lanes == 0, gain, shift).T
    norms = jnp.concatenate([norms_ref[...]] * 2, 0).T
    product = (product * norms[:, 0:1] + norms[:, 1:2] * bias).astype(B)
    sums = jnp.concatenate([ones[:2], two_ref[...]], 0).astype(B)
    bias = bias.astype(B)
    for block in range(blocks):
        out_ref[block, :depth, :] = product[block * depth : (block + 1) * depth]
        mine = sums[:, block * norm_size : (block + 1) * norm_size]
        out_ref[block, depth:, :] = jnp.concatenate(
            [
                jnp.concatenate([mine, jnp.zeros((4, columns - norm_size), B)], 1),
                bias,
                jnp.zeros((rows - depth - 5, columns), B),
            ],
            0,
        )


def weights_back(hat_all, grad_proj, w_mine, norms, two, bias_grad, depth, norm_size):
    tokens, features = hat_all.shape
    columns = grad_proj.shape[1]
    block = min(512, features)
    flat = lambda array: pl.BlockSpec(array.shape, lambda i: (0, 0))
    across = lambda rows: pl.BlockSpec((rows, block), lambda i: (0, i))
    return pl.pallas_call(
        functools.partial(weights_back_body, depth, norm_size),
        grid=(features // block,),
        in_specs=[
            across(tokens),
            flat(grad_proj),
            row_spec(columns, block),
            across(4),
            across(2),
            flat(bias_grad),
        ],
        out_specs=pl.BlockSpec((block // depth, depth + EXTRA_ROWS, columns), lambda i: (i, 0, 0)),
        out_shape=jax.ShapeDtypeStruct((features // depth, depth + EXTRA_ROWS, columns), B),
        name="weights_back",
        cost_estimate=cost(tokens * features * columns, 4 * tokens * features),
    )(hat_all, grad_proj, w_mine, norms, two, bias_grad)


def norm_back_body(e_ref, x_ref, upstream_ref, gain_ref, grad_ref, *refs):
    hat, inverse = unit_rows(x_ref[...].astype(F))
    e = e_ref[...].astype(F)
    scaled = e * gain_ref[...]
    mean_grad = jnp.mean(scaled, axis=-1, keepdims=True)
    mean_proj = jnp.mean(scaled * hat, axis=-1, keepdims=True)
    grad = upstream_ref[...].astype(F) + inverse * (scaled - mean_grad - hat * mean_proj)
    grad_ref[...] = grad
    if refs:
        rounded_ref, sums_ref = refs
        rounded_ref[...] = grad.astype(B)
        sums = jnp.concatenate(
            [jnp.sum(e * hat, axis=0, keepdims=True), jnp.sum(e, axis=0, keepdims=True)], 0
        )

        @pl.when(pl.program_id(0) == 0)
        def _():
            sums_ref[...] = sums

        @pl.when(pl.program_id(0) != 0)
        def _():
            sums_ref[...] += sums


def norm_back(e, x, upstream, gain, more):
    tokens, features = x.shape
    outs = [jax.ShapeDtypeStruct((tokens, features), F)]
    if more:
        outs += [jax.ShapeDtypeStruct((tokens, features), B), jax.ShapeDtypeStruct((2, features), F)]
    block = min(64, tokens)
    rows = row_spec(features, block)
    sums = pl.BlockSpec((2, features), lambda i: (0, 0))
    return pl.pallas_call(
        norm_back_body,
        grid=(tokens // block,),
        in_specs=[rows, rows, rows, whole_spec(gain)],
        out_specs=[rows, rows, sums] if more else [rows],
        out_shape=outs,
        name="norm_back",
    )(e, x, upstream, gain)


def pack_body(strided, me_ref, w_ref, norm_ref, bias_ref, out_ref):
    wide, _, columns = out_ref.shape
    depth = w_ref.shape[0]
    third = w_ref.shape[1] // 3
    width = columns // 3
    me = me_ref[0]
    held = bias_ref.shape[1]
    padded = jnp.concatenate(
        [norm_ref[...], jnp.zeros((4, columns - norm_ref.shape[1]), B)], 1
    )
    for owner in range(wide):
        biases = []
        for part in range(3):
            for slot in range(width // HEAD_DIM):
                head = slot * wide + owner if strided else owner * (width // HEAD_DIM) + slot
                first = part * third + head * HEAD_DIM
                if slot % 2 == 0:
                    left = w_ref[:, first : first + HEAD_DIM]
                else:
                    to = part * width + (slot - 1) * HEAD_DIM
                    out_ref[owner, :depth, to : to + 2 * HEAD_DIM] = jnp.concatenate(
                        [left, w_ref[:, first : first + HEAD_DIM]], 1
                    )
                last = first + HEAD_DIM
                while first < last:
                    stop = min(last, (first // held + 1) * held)
                    mine = bias_ref[:, first % held : first % held + stop - first]
                    kept = jnp.where(me == first // held, mine.astype(F), 0.0)
                    biases.append(kept.astype(B))
                    first = stop
        out_ref[owner, depth:, :] = jnp.concatenate(
            [padded, jnp.concatenate(biases, 1), jnp.zeros((EXTRA_ROWS - 5, columns), B)], 0
        )


def pack(me, w_qkv, norm_params, b_qkv, strided, wide):
    depth, columns = w_qkv.shape
    memory = [pltpu.SMEM] + [pltpu.VMEM] * 3
    return pl.pallas_call(
        functools.partial(pack_body, strided),
        in_specs=[pl.BlockSpec(memory_space=space) for space in memory],
        out_shape=jax.ShapeDtypeStruct((wide, depth + EXTRA_ROWS, columns // wide), B),
        name="pack",
    )(me[None].astype(jnp.int32), w_qkv, norm_params, b_qkv[None])


def adam_step(parameter, gradient, moments):
    first_moment = BETA_ONE * moments[0] + (1.0 - BETA_ONE) * gradient
    second_moment = BETA_TWO * moments[1] + (1.0 - BETA_TWO) * gradient * gradient
    return first_moment / BIAS_FIRST / (
        jnp.sqrt(second_moment / BIAS_SECOND) + ADAM_EPS
    ) + DECAY_RATE * parameter.astype(F)


def finish_body(strided, wide, got_ref, w_ref, moment_ref, grad_ref, step_ref):
    depth, third = w_ref.shape
    width = got_ref.shape[2]
    for at in range(third // 128):
        if strided:
            slot, owner = at * 2 // wide, at * 2 % wide
            first = slot * HEAD_DIM
            gradient = jnp.concatenate(
                [got_ref[owner + k, :depth, first : first + HEAD_DIM] for k in range(2)], 1
            )
        else:
            owner, first = at * 128 // width, at * 128 % width
            gradient = got_ref[owner, :depth, first : first + 128]
        gradient = gradient.astype(F)
        columns = slice(at * 128, at * 128 + 128)
        grad_ref[:, columns] = gradient
        step_ref[:, columns] = adam_step(
            w_ref[:, columns], gradient, (moment_ref[0, :, columns], moment_ref[1, :, columns])
        )


def finish(received, w_qkv, moments, strided):
    wide, rows, columns = received.shape
    depth = w_qkv.shape[0]
    third = w_qkv.shape[1] // 3
    part = pl.BlockSpec((depth, third), lambda i: (0, i))
    return pl.pallas_call(
        functools.partial(finish_body, strided, wide),
        grid=(3,),
        in_specs=[
            pl.BlockSpec((wide, rows, columns // 3), lambda i: (0, 0, i)),
            part,
            pl.BlockSpec((2, depth, third), lambda i: (0, 0, i)),
        ],
        out_specs=[part, part],
        out_shape=[jax.ShapeDtypeStruct(w_qkv.shape, F)] * 2,
        name="finish",
    )(received, w_qkv, moments)


def shards(
    block_input, out_grad, segment_ids, positions, norm_params, w_qkv, b_qkv, w_out, gate_up, w_down,
    moment_norm, moment_qkv, moment_bias, moment_out, moment_gate, moment_down,
):
    x_own = block_input[0]
    local_len, features = x_own.shape
    rows = lax.axis_size("rows")
    wide = lax.axis_size("wide")
    my_row = lax.axis_index("rows")
    my_wide = lax.axis_index("wide")
    segment_row = segment_ids[0]
    heads = HEADS // wide
    width = heads * HEAD_DIM
    depth = w_qkv.shape[0]
    norm_size = norm_params.shape[1]
    strided = depth == HEAD_DIM

    bias_size = b_qkv.shape[0]
    chips = wide // 2
    core = my_wide % 2
    blocks = range(rows * wide)
    back = [(b % rows * wide + b // rows, b) for b in blocks]
    gate_first = gate_up.swapaxes(1, 2)
    packed = pack(my_row * wide + my_wide, w_qkv, norm_params, b_qkv, strided, wide)
    packed, gate_shard = tie(packed, gate_first[0])
    gate = RowsGather(gate_shard, 1)
    exchange = WideExchange(packed)
    segment_row, *arrived = exchange.before(segment_row, *(gate.step or ()))
    gate.step = arrived or None
    received, x_first = tie(exchange.join(), x_own)
    x_all = wide_gather(x_first)
    w_rows = RowsGather(received, 0)
    seg_col = segment_row[:, None]
    seg_line = segment_row[None, :]
    tables = w_rows.before(*rotary_tables(seg_col, seg_line))
    w_rows.second()
    if gate.step:
        up_first, *gate.step = w_rows.before(gate_first[1], *gate.step)
    else:
        up_first = gate_first[1]
    x_all, up_first = tie(gate.halves(x_all), up_first)
    up = RowsGather(up_first, 1)
    gate.second()
    if strided:
        x_all, out_first = w_rows.before(x_all, w_out)
        out_line = lax.all_gather(out_first, "wide", axis=0, tiled=False)
    q, k, v, hat_all, w_mine, norms, _ = project(x_all, w_rows, tables, depth, norm_size)
    attended, lse = attend(q, k, v, seg_col, seg_line, heads)
    attended = gate.before(up.before(attended))
    if strided:
        attended, out_line = tie(attended, out_line)
    attended_all = lax.all_gather(attended, "wide", axis=0, tiled=False)
    if strided:
        out_line = out_line.reshape(chips, 2, depth, features)
        out_line = lax.dynamic_index_in_dim(out_line, core, 1, False)
        out_rows = RowsGather(out_line.reshape(chips * depth, features), 0)
        out_rows.second()
        out_rows.step = up.before(*out_rows.step) if out_rows.step else None
        out_pieces, out_places = out_rows.pieces()
    else:
        out_all = lax.all_gather(w_out, ("rows", "wide"), axis=0, tiled=True)
        out_all = out_all.reshape(chips, 2, width, features)
        out_line = lax.dynamic_index_in_dim(out_all, core, 1, False)
        out_pieces, out_places = [out_line.reshape(chips * width, features)], [jnp.int32(0)]
    swapped = [core_swap(piece) for piece in out_pieces]
    norms_two = norms[2:]
    attended_all = up.halves(attended_all)
    up.second()
    attended_all, upstream, down_first, norms_two, *swapped = tie(
        attended_all, out_grad[0], w_down, norms_two, *swapped
    )
    down = RowsGather(down_first, 1)
    grads_all = wide_gather(upstream)
    tokens_all, after_all, out_mine = out_project(
        (core, my_wide // 2), attended_all, out_pieces, swapped, out_places, x_all, norms_two
    )
    tokens_all = down.before(tokens_all)
    down.second()
    after_attn = lax.dynamic_slice_in_dim(after_all, my_wide * local_len, local_len, 0)
    gate_part, up_part, hidden = gate_up_forward(tokens_all, gate, up)

    gate_grads, e_two = feed_back(grads_all, gate_part, up_part, down, gate, up)
    grad_normed_two = wide_scatter(e_two)
    gate_grads, hidden, tokens_all, grads_all = tie(gate_grads, hidden, tokens_all, grads_all)
    gate_grad = jnp.einsum("gtf,td->gfd", gate_grads, tokens_all, preferred_element_type=F).astype(B)
    down_grad = jnp.einsum("tf,td->fd", hidden, grads_all, preferred_element_type=F).astype(B)
    grad_down = RowsSum(down_grad, 1)
    grad_gate = RowsSum(gate_grad, 2)
    grad_normed_two = grad_gate.before(grad_down.before(grad_normed_two))
    hidden, *_ = tie(hidden, *grad_down.second(), *grad_gate.second())
    mlp_part = down_forward(hidden, down, features)

    grad_after, branch, sums_two = norm_back(
        grad_normed_two, after_attn, out_grad[0], norms[2:3], True
    )
    branch_all = wide_gather(branch)
    mlp_part, branch_all = grad_gate.after(mlp_part, branch_all)
    mlp_out = wide_scatter(mlp_part)
    grad_attended = dotg(branch_all, out_mine, NT).astype(B)
    grad_proj, bias_grad = attend_back(
        q, k, v, grad_attended, lse, seg_col, seg_line, tables, heads
    )
    grad_proj = grad_down.after(grad_proj)
    e_one = dotg(grad_proj, w_mine, NT).astype(B)
    e_one, grad_proj, branch_all = tie(e_one, grad_proj, branch_all)
    grad_normed_one = wide_scatter(e_one)
    grad_out = RowsSum(dotg(attended, branch_all, TN).astype(B), 0)
    packed = weights_back(
        hat_all, grad_proj, w_mine, norms, sums_two, bias_grad, depth, norm_size
    )
    qkv_sum = RowsSum(packed, 0)
    qkv_sum.whole = grad_out.before(qkv_sum.whole)
    grad_out.second()
    start = no_change(qkv_sum.second()[0])
    mlp_out = qkv_sum.after(mlp_out)
    exchange = WideExchange(qkv_sum.result().astype(B))
    grad_out = grad_out.result() + start
    if not strided:
        grad_out = lax.ppermute(grad_out.astype(B), ("rows", "wide"), back).astype(F)
    grad_down = grad_down.result() + start
    grad_gate = (grad_gate.result() + start).swapaxes(1, 2)
    step_out = adam_step(w_out, grad_out, moment_out)
    step_gate = adam_step(gate_up, grad_gate, moment_gate)
    step_down = adam_step(w_down, grad_down, moment_down)
    received = exchange.join()

    block_out = (after_attn + mlp_out.astype(F)).astype(B)
    grad_qkv, step_qkv = finish(received, w_qkv, moment_qkv, strided)
    grad_qkv, step_qkv, grad_normed_one = tie(grad_qkv, step_qkv, grad_normed_one)
    input_grad = norm_back(grad_normed_one, x_own, grad_after, norms[0:1], False)[0]
    extra = received[:, depth : depth + 5].astype(F)
    grad_norms = jnp.sum(extra[:, :4, :norm_size], axis=0)
    bias_all = extra[:, 4].reshape(wide, 3, heads, HEAD_DIM)
    bias_all = bias_all.transpose((1, 2, 0, 3) if strided else (1, 0, 2, 3)).reshape(-1)
    grad_bias = lax.dynamic_slice_in_dim(
        bias_all, (my_row * wide + my_wide) * bias_size, bias_size, 0
    )

    return (
        block_out[None],
        input_grad[None],
        grad_norms,
        grad_qkv,
        grad_bias,
        grad_out,
        grad_gate,
        grad_down,
        adam_step(norm_params, grad_norms, moment_norm),
        step_qkv,
        adam_step(b_qkv, grad_bias, moment_bias),
        step_out,
        step_gate,
        step_down,
    )


def solution(mesh):
    both = ("rows", "wide")
    tokens = P("rows", "wide", None)
    weights = (P(None, both), P(both, None), P(both), P(both, None), P(None, "rows", "wide"), P("wide", "rows"))
    moments = tuple(P(None, *spec) for spec in weights)
    return jax.shard_map(
        shards,
        mesh=mesh,
        in_specs=(tokens, tokens, P("rows", None), P("rows", "wide")) + weights + moments,
        out_specs=(tokens, tokens) + weights + weights,
        check_vma=False,
    )
```
